128 devices in a mesh: vid: 4 (over z_lo, core), tm: 32 (over x, z_hi, y).
Axes of the slice: x: 4, y: 4, z: 4 (z_hi: 2, z_lo: 2; z = z_hi * 2 + z_lo), core: 2. Of those that a mesh axis runs over, the one named last changes fastest.
Arguments:
- video: bfloat16 [4, 8192, 2048], P('vid', 'tm'), may hold values from -6 to 6
- norm_gain: bfloat16 [2048], replicated, may hold values from 0.099609375 to 1.8984375
- query_weight: bfloat16 [2048, 1024], P(('vid', 'tm')), may hold values from -6 to 6
- key_weight: bfloat16 [2048, 1024], P(('vid', 'tm')), may hold values from -0.125 to 0.125
- value_weight: bfloat16 [2048, 1024], P(('vid', 'tm')), may hold values from -0.125 to 0.125
- key_kernel: bfloat16 [27, 1024], replicated, may hold values from -1.25 to 1.25
- value_kernel: bfloat16 [27, 1024], replicated, may hold values from -1.25 to 1.25
- out_weight: bfloat16 [1024, 2048], P(('vid', 'tm')), may hold values from -0.1875 to 0.1875
- frames_valid: int32 [4], replicated, may hold values from 64 to 128, as said below
Outputs:
- attended: bfloat16 [4, 8192, 2048], P('vid', 'tm')
The draws below stay inside these ranges and needn't reach their ends.
Inputs may be any that keep to these rules, and one draw needn't show every extreme that they name: `frames_valid`: one video has all 128 frames valid.
All inputs are finite; a program needn't handle non-finite values.
Results may differ from the reference program's by a relative error of at most 0.006.
The reference program's roundings to bfloat16 on the way (of `normed`, `pooled_key`, `pooled_value` and `heads`) count: a program that leaves them out, or rounds other values in their place, can miss the bound.
Values may be sent and summed in bfloat16 or wider, within the bound.
A program may use at most 64 MiB of HBM per device.

```python
import math
import jax
import jax.numpy as jnp
from jax import lax

D = 2048
HEADS = 8
HD = 128
SIDE = 8
TOK_DEV = 256
MEM_DEV = 32
FRAMES = 128
TLEN = 8192
MEMORY = 1024
NV = 4
N_TM = 32


def draw_query_weight(key, part):
    first = jax.random.fold_in(jax.random.fold_in(key, 11), 0)
    base = jnp.clip(jax.random.normal(first, (D, HEADS * HD), jnp.float32), -6.0, 6.0) * D ** (-0.5)
    return jnp.clip(base, -6.0, 6.0).astype(jnp.bfloat16)


def draw_frames_valid(key, part):
    first, second = jax.random.split(jax.random.fold_in(key, 23))
    counts = jax.random.randint(first, (NV,), FRAMES // 2, FRAMES + 1)
    chosen = jax.random.randint(second, (), 0, NV)
    return jnp.where(jnp.arange(NV) == chosen, FRAMES, counts).astype(jnp.int32)


def levels(key, extent, pieces, smallest, high):
    def one(dim, shards_of):
        steps = jax.random.uniform(jax.random.fold_in(jax.random.fold_in(key, 6), dim), (shards_of,), jnp.float32, smallest / len(pieces), high / len(pieces))
        return jnp.repeat(jnp.exp(steps), extent[dim] // shards_of).reshape((-1,) + (1,) * (len(extent) - dim - 1))

    factor_of = one(*pieces[0])
    for cut in pieces[1:]:
        factor_of = factor_of * one(*cut)
    return factor_of


def noise(key, shape, deviation, most, shards=(), kind=jnp.bfloat16):
    array = deviation * jax.random.normal(key, shape, jnp.float32)
    if shards:
        array = array * levels(key, shape, shards, -0.22, 0.18)
    return jnp.clip(array, -most, most).astype(kind)


def setup_inputs(seed: int = 0) -> dict:
    keys = jax.random.split(jax.random.key(seed), 10)
    return {
        "video": noise(keys[0], (NV, TLEN, D), 1.0, 6.0, ((0, 4), (1, 32))),
        "norm_gain": jnp.clip(1.0 + 0.18 * jax.random.normal(keys[1], (D,), jnp.float32), 0.099609375, 1.8984375).astype(jnp.bfloat16),
        "query_weight": draw_query_weight(jax.random.fold_in(keys[9], 71), 0),
        "key_weight": noise(keys[3], (D, HEADS * HD), D ** -0.5, 0.125, ((0, 128),)),
        "value_weight": noise(keys[4], (D, HEADS * HD), D ** -0.5, 0.125, ((0, 128),)),
        "key_kernel": noise(keys[5], (27, HEADS * HD), 27 ** -0.5, 1.25),
        "value_kernel": noise(keys[6], (27, HEADS * HD), 27 ** -0.5, 1.25),
        "out_weight": noise(keys[7], (HEADS * HD, D), (HEADS * HD) ** -0.5, 0.1875, ((0, 128),)),
        "frames_valid": draw_frames_valid(jax.random.fold_in(keys[9], 71), 0),
    }


def normalize(rows, gain):
    values = rows.astype(jnp.float32)
    center = lax.optimization_barrier(jnp.mean(values, axis=-1, keepdims=True))
    spread = lax.optimization_barrier(jnp.mean((values - center) ** 2, axis=-1, keepdims=True))
    return ((values - center) * lax.rsqrt(spread + 1e-06) * gain.astype(jnp.float32)).astype(jnp.bfloat16)

def pool_frames(frames, previous, kernel):
    count, side = (frames.shape[0], frames.shape[1])
    width = frames.shape[3]
    half_f, half_s = (count // 2, side // 2)
    stacked = jnp.concatenate([previous[None], frames], axis=0).astype(jnp.float32)
    padded = jnp.pad(stacked, ((0, 0), (1, 1), (1, 1), (0, 0)))
    taps = kernel.astype(jnp.float32)
    total = jnp.zeros((half_f, half_s, half_s, width), jnp.float32)
    for step_t in range(3):
        for step_h in range(3):
            for step_w in range(3):
                piece = padded[2 - step_t:2 - step_t + 2 * half_f - 1:2, step_h:step_h + 2 * half_s - 1:2, step_w:step_w + 2 * half_s - 1:2]
                total = total + piece * taps[9 * step_t + 3 * step_h + step_w]
    grouped = total.reshape(half_f * half_s * half_s, HEADS, width // HEADS)
    center = lax.optimization_barrier(jnp.mean(grouped, axis=-1, keepdims=True))
    spread = lax.optimization_barrier(jnp.mean((grouped - center) ** 2, axis=-1, keepdims=True))
    normed = (grouped - center) * lax.rsqrt(spread + 1e-06)
    return normed.reshape(half_f * half_s * half_s, width).astype(jnp.bfloat16)

def reference(video, norm_gain, query_weight, key_weight, value_weight, key_kernel, value_kernel, out_weight, frames_valid):
    spatial = SIDE * SIDE
    width = HEADS * HD
    scale = 1.0 / math.sqrt(HD)

    def one_video(inputs):
        tokens, limit = inputs
        normed = normalize(tokens, norm_gain)
        query = jnp.dot(normed, query_weight, preferred_element_type=jnp.float32).astype(jnp.bfloat16)
        key = jnp.dot(normed, key_weight, preferred_element_type=jnp.float32).astype(jnp.bfloat16)
        value = jnp.dot(normed, value_weight, preferred_element_type=jnp.float32).astype(jnp.bfloat16)
        frame = jnp.arange(TLEN, dtype=jnp.int32) // spatial
        valid = frame < limit
        zero = jnp.zeros_like(key)
        masked_key = jnp.where(valid[:, None], key, zero)
        masked_value = jnp.where(valid[:, None], value, zero)
        blank = jnp.zeros((SIDE, SIDE, width), jnp.bfloat16)
        pooled_key = pool_frames(masked_key.reshape(FRAMES, SIDE, SIDE, width), blank, key_kernel)
        pooled_value = pool_frames(masked_value.reshape(FRAMES, SIDE, SIDE, width), blank, value_kernel)
        mem_index = jnp.arange(MEMORY, dtype=jnp.int32)
        mem_frame = mem_index // (spatial // 4)
        mem_valid = 2 * mem_frame < limit
        mem_source = mem_index // MEM_DEV
        mem_keys = pooled_key.reshape(MEMORY, HEADS, HD).astype(jnp.float32)
        mem_values = pooled_value.reshape(MEMORY, HEADS, HD).astype(jnp.float32)

        def one_block(block):
            begin = (block * TOK_DEV).astype(jnp.int32)
            qb = lax.dynamic_slice_in_dim(query, begin, TOK_DEV, 0).reshape(TOK_DEV, HEADS, HD).astype(jnp.float32)
            kb = lax.dynamic_slice_in_dim(key, begin, TOK_DEV, 0).reshape(TOK_DEV, HEADS, HD).astype(jnp.float32)
            vb = lax.dynamic_slice_in_dim(value, begin, TOK_DEV, 0).reshape(TOK_DEV, HEADS, HD).astype(jnp.float32)
            fb = lax.dynamic_slice_in_dim(frame, begin, TOK_DEV, 0)
            okb = lax.dynamic_slice_in_dim(valid, begin, TOK_DEV, 0)
            local_ok = (fb[None, :] <= fb[:, None]) & okb[None, :]
            local_scores = jnp.einsum('qhd,khd->hqk', qb, kb) * scale
            local_scores = jnp.where(local_ok[None], local_scores, -1e+30)
            mem_ok = mem_valid & (mem_source <= block)
            mem_scores = jnp.einsum('qhd,khd->hqk', qb, mem_keys) * scale
            mem_scores = jnp.where(mem_ok[None, None, :], mem_scores, -1e+30)
            scores = jnp.concatenate([local_scores, mem_scores], axis=-1)
            top = lax.optimization_barrier(jnp.max(scores, axis=-1, keepdims=True))
            weights = jnp.exp(scores - top)
            total = lax.optimization_barrier(jnp.sum(weights, axis=-1))
            both = jnp.concatenate([vb, mem_values], axis=0)
            mixed = jnp.einsum('hqk,khd->hqd', weights, both, precision=lax.Precision.HIGHEST) / total[..., None]
            heads = jnp.transpose(mixed, (1, 0, 2)).reshape(TOK_DEV, width).astype(jnp.bfloat16)
            result = jnp.dot(heads, out_weight, preferred_element_type=jnp.float32)
            return jnp.where(okb[:, None], result, 0.0).astype(jnp.bfloat16)
        blocks = lax.map(one_block, jnp.arange(N_TM, dtype=jnp.int32))
        return blocks.reshape(TLEN, D)
    return lax.map(one_video, (video, frames_valid))
```

```python
import functools
import math

import jax
import jax.numpy as jnp
from jax import lax
from jax.experimental import pallas as pl
from jax.experimental.pallas import tpu as pltpu
from jax.sharding import PartitionSpec as P

MESH = pl.DeviceIdType.MESH
HEADS = 8
HD = 128
SIDE = 8
SPATIAL = SIDE * SIDE
N_TM = 32
ROWS = 256
FRAMES_DEV = ROWS // SPATIAL
EXT = ROWS + SPATIAL
MEM_DEV = 32
D = 2048
WIDTH = HEADS * HD
NEG = -1e30
SCALE = (1.0 / math.sqrt(HD)) * math.log2(math.e)

STREAMS = (
    (
        (1, 0, 768, "xyz"),
        (1, 768, 256, "yzx"),
        (2, 0, 384, "yzx"),
        (2, 384, 640, "zxy"),
    ),
    (
        (0, 0, 640, "xyz"),
        (0, 640, 384, "yzx"),
        (3, 0, 512, "yzx"),
        (3, 512, 1536, "zxy"),
    ),
)
PIECES = STREAMS[0] + STREAMS[1]
MEMORY_ORDERS = ("xy", "yx")


def device(place, core):
    x, y, z = place["x"], place["y"], place["z"]
    return (lax.rem(z, 2) * 2 + core, x * 8 + (z // 2) * 4 + y)


def moved(place, axis, steps):
    return {**place, axis: lax.rem(place[axis] + steps + 4, 4)}


def halves(start, size):
    first = (size // 256) * 128 if size > 128 else size
    first = size - first
    return ((start, first), (start + first, size - first))


class Wires:
    def __init__(self, send_sems, recv_sems):
        self.send_sems, self.recv_sems = send_sems, recv_sems
        self.count = 0
        self.started = []

    def slot(self):
        self.count += 1
        return self.count - 1

    def send(self, slot, src, dst, target):
        copy = pltpu.make_async_remote_copy(
            src_ref=src,
            dst_ref=dst,
            send_sem=self.send_sems.at[slot],
            recv_sem=self.recv_sems.at[slot],
            device_id=target,
            device_id_type=MESH,
        )
        copy.start()
        self.started.append(copy)

    def receive(self, slot, dst, source):
        pltpu.make_async_remote_copy(
            src_ref=dst,
            dst_ref=dst,
            send_sem=self.send_sems.at[slot],
            recv_sem=self.recv_sems.at[slot],
            device_id=source,
            device_id_type=MESH,
        ).wait_recv()

    def drain(self):
        for copy in self.started:
            copy.wait_send()


def weight_view(ref, core, place, start, size):
    every = slice(None)
    x, y, z = (place[axis] for axis in "xyz")
    zl = every if z is None else lax.rem(z, 2)
    zh = every if z is None else z // 2
    return ref.at[
        zl,
        core,
        every if x is None else x,
        zh,
        every if y is None else y,
        :,
        pl.ds(start, size),
    ]


def memory_view(ref, place, start, size):
    every = slice(None)
    x, y, z = (place[axis] for axis in "xyz")
    return ref.at[
        every if x is None else x,
        every if z is None else z // 2,
        every if y is None else y,
        :,
        pl.ds(start, size),
    ]


class Ring:
    def __init__(self, wires, view, place, core, axis, known, start, size):
        self.wires, self.place, self.core, self.axis = wires, place, core, axis
        self.known, self.start, self.size = known, start, size
        self.view = view
        self.slots = [wires.slot() for _ in range(4)]

    def region(self, steps, start, size):
        place = {**moved(self.place, self.axis, steps), **{a: None for a in self.known}}
        return self.view(place, start, size)

    def target(self, steps):
        return device(moved(self.place, self.axis, steps), self.core)

    def open(self, src=None):
        mine = self.region(0, self.start, self.size)
        for slot, steps in zip(self.slots[:2], (1, -1)):
            self.wires.send(slot, mine if src is None else src, mine, self.target(steps))

    def relay(self):
        for slot, steps, part in zip(self.slots[:2], (1, -1), halves(self.start, self.size)):
            self.wires.receive(slot, self.region(-steps, self.start, self.size), self.target(-steps))
        for slot, steps, part in zip(self.slots[2:], (1, -1), halves(self.start, self.size)):
            region = self.region(-steps, *part)
            self.wires.send(slot, region, region, self.target(steps))

    def close(self):
        for slot, steps, part in zip(self.slots[2:], (1, -1), halves(self.start, self.size)):
            self.wires.receive(slot, self.region(2, *part), self.target(-steps))


class Gather:
    def __init__(self, wires, ref, shard, place, core, piece):
        _, self.start, self.size, order = piece
        self.wires, self.ref, self.shard = wires, ref, shard
        self.place, self.core, self.order = place, core, order
        self.partner = device(place, 1 - core)
        self.rings = [
            Ring(
                wires,
                lambda at, start, size: weight_view(ref, core, at, start, size),
                place,
                core,
                axis,
                order[:k],
                self.start,
                self.size,
            )
            for k, axis in enumerate(order)
        ]
        self.slots = [wires.slot() for _ in range(4)]

    def open(self):
        self.rings[0].open(self.shard.at[:, pl.ds(self.start, self.size)])

    def relay(self, k):
        self.rings[k].relay()

    def close(self, k):
        self.rings[k].close()
        if k < 2:
            self.rings[k + 1].open()

    def region(self, core, steps):
        place = {
            **moved(self.place, self.order[2], steps),
            self.order[0]: None,
            self.order[1]: None,
        }
        return weight_view(self.ref, core, place, self.start, self.size)

    def hand(self, k):
        region = self.region(self.core, (0, 1, -1, 2)[k])
        self.wires.send(self.slots[k], region, region, self.partner)

    def take(self):
        for k, steps in enumerate((0, 1, -1, 2)):
            self.wires.receive(self.slots[k], self.region(1 - self.core, steps), self.partner)


def normalize_rows(values, gain):
    center = jnp.mean(values, axis=-1, keepdims=True)
    spread = jnp.mean((values - center) ** 2, axis=-1, keepdims=True)
    return ((values - center) * lax.rsqrt(spread + 1e-06) * gain).astype(jnp.bfloat16)


def project(normed, first, count, weight, out):
    def tile(j, carry):
        columns = pl.ds(pl.multiple_of(j * 256, 256), 256)
        total = jnp.zeros((count, 256), jnp.float32)
        for vid in range(4):
            rows = weight[vid // 2, vid % 2, :, :, :, :, columns].reshape(512, 256)
            total = total + jnp.dot(
                normed[first : first + count, vid * 512 : (vid + 1) * 512],
                rows,
                preferred_element_type=jnp.float32,
            )
        out[:, columns] = total.astype(jnp.bfloat16)
        return carry

    lax.fori_loop(0, WIDTH // 256, tile, 0)


def pool(source, taps, valid, spread_tmp, out, place):
    column = lax.broadcasted_iota(jnp.int32, (SIDE, HD), 0)

    def head(h, carry):
        lanes = pl.ds(pl.multiple_of(h * HD, HD), HD)
        grid = source[:, lanes].astype(jnp.float32).reshape(FRAMES_DEV + 1, SIDE, SIDE, HD)
        kernel = taps[:, lanes].astype(jnp.float32)
        frames = [jnp.where(valid[f], grid[f], 0.0) for f in range(FRAMES_DEV + 1)]
        for j in range(FRAMES_DEV // 2):
            for a in range(SIDE // 2):
                sums = [jnp.zeros((SIDE, HD), jnp.float32) for _ in range(3)]
                for dt in range(3):
                    for dh in range(3):
                        row = 2 * a + dh - 1
                        if row < 0:
                            continue
                        values = frames[2 * j + 2 - dt][row]
                        for dw in range(3):
                            tap = 9 * dt + 3 * dh + dw
                            sums[dw] = sums[dw] + values * kernel[tap : tap + 1]
                left = jnp.where(column == 0, 0.0, pltpu.roll(sums[0], 1, 0))
                right = pltpu.roll(sums[2], SIDE - 1, 0)
                at = (j * (SIDE // 2) + a) * SIDE
                spread_tmp[h, at : at + SIDE, :] = sums[1] + left + right
        rows = spread_tmp[h, pl.ds(0, MEM_DEV, stride=2), :]
        center = jnp.mean(rows, axis=-1, keepdims=True)
        width = jnp.mean((rows - center) ** 2, axis=-1, keepdims=True)
        normed = (rows - center) * lax.rsqrt(width + 1e-06)
        out[place["x"], place["z"] // 2, place["y"], :, lanes] = normed.astype(jnp.bfloat16)
        return carry

    lax.fori_loop(0, HEADS, head, 0)


def scores_of(queries, keys):
    return lax.dot_general(
        queries, keys, (((1,), (1,)), ((), ())), preferred_element_type=jnp.float32
    )


def weighted(weights, values):
    high = weights.astype(jnp.bfloat16)
    low = (weights - high.astype(jnp.float32)).astype(jnp.bfloat16)
    return jnp.dot(high, values, preferred_element_type=jnp.float32) + jnp.dot(
        low, values, preferred_element_type=jnp.float32
    )


def body(
    video,
    gain,
    query_shard,
    key_shard,
    value_shard,
    key_taps,
    value_taps,
    out_shard,
    frames_valid,
    out,
    tokens,
    normed,
    query_w,
    key_w,
    value_w,
    out_w,
    out_rows,
    query,
    key,
    value,
    memory_key,
    memory_value,
    spread_key,
    spread_value,
    heads,
    local_sems,
    send_sems,
    recv_sems,
):
    vid, tm = lax.axis_index("vid"), lax.axis_index("tm")
    core = lax.rem(vid, 2)
    place = {
        "x": tm // 8,
        "y": lax.rem(tm, 4),
        "z": lax.rem(tm // 4, 2) * 2 + vid // 2,
    }
    after, before = lax.rem(tm + 1, N_TM), lax.rem(tm + N_TM - 1, N_TM)
    partner = device(place, 1 - core)
    across = device(moved(place, "z", 2), core)

    barrier = pltpu.get_barrier_semaphore()
    greeted = [device(moved(place, axis, steps), core) for axis in "xyz" for steps in (1, -1)]
    greeted += [partner, across, (vid, after), (vid, before)]
    for other in greeted:
        pl.semaphore_signal(barrier, inc=1, device_id=other, device_id_type=MESH)

    shards = (query_shard, key_shard, value_shard, out_shard)
    weights = (query_w, key_w, value_w, out_w)
    own = [
        pltpu.make_async_copy(
            shard,
            weight.at[vid // 2, core, place["x"], place["z"] // 2, place["y"]],
            local_sems.at[k],
        )
        for k, (shard, weight) in enumerate(zip(shards, weights))
    ]
    own_tokens = pltpu.make_async_copy(video, tokens.at[pl.ds(SPATIAL, ROWS)], local_sems.at[4])
    for copy in own:
        copy.start()
    own_tokens.start()
    pl.semaphore_wait(barrier, len(greeted))

    wires = Wires(send_sems, recv_sems)
    streams = [
        [Gather(wires, weights[p[0]], shards[p[0]], place, core, p) for p in stream]
        for stream in STREAMS
    ]
    for stream in streams:
        for gather in stream:
            gather.open()
    halo_slot = wires.slot()
    halo = tokens.at[pl.ds(0, SPATIAL)]
    wires.send(halo_slot, video.at[pl.ds(ROWS - SPATIAL, SPATIAL)], halo, (vid, after))
    for copy in own:
        copy.wait()
    own_tokens.wait()

    scale = gain[...].astype(jnp.float32)

    def normalize_at(i, carry):
        at = pl.ds(pl.multiple_of(i * 32, 32), 32)
        normed[at, :] = normalize_rows(tokens[at, :].astype(jnp.float32), scale)
        return carry

    for k in range(3):
        for stream in streams:
            for gather in stream:
                gather.relay(k)
        if k == 0:
            lax.fori_loop(SPATIAL // 32, EXT // 32, normalize_at, 0)
        if k == 1:
            wires.receive(halo_slot, halo, (vid, before))
            lax.fori_loop(0, SPATIAL // 32, normalize_at, 0)
        if k == 2:
            for stream in streams:
                for gather in stream:
                    gather.hand(0)
                    gather.hand(1)
                    gather.hand(2)
        for number, stream in enumerate(streams):
            for gather in stream:
                gather.close(k)
            if k == 2:
                for gather in stream:
                    gather.hand(3)
                for gather in stream:
                    gather.take()
                if number == 0:
                    project(normed, 0, EXT, key_w, key)
                    project(normed, 0, EXT, value_w, value)
                else:
                    project(normed, SPATIAL, ROWS, query_w, query)

    limit = frames_valid[vid]
    first_frame = tm * FRAMES_DEV
    valid = [
        (first_frame + f - 1 < limit) & (first_frame + f - 1 >= 0) for f in range(FRAMES_DEV + 1)
    ]
    pool(key, key_taps, valid, spread_key, memory_key, place)
    pool(value, value_taps, valid, spread_value, memory_value, place)

    memory = []
    for ref, order in zip((memory_key, memory_value), MEMORY_ORDERS):
        region = memory_view(ref, place, 0, WIDTH)
        slot = wires.slot()
        wires.send(slot, region, region, across)
        rings = [
            Ring(
                wires,
                functools.partial(
                    lambda at_ref, at, start, size: memory_view(at_ref, at, start, size), ref
                ),
                place,
                core,
                axis,
                "z" + order[:k],
                0,
                WIDTH,
            )
            for k, axis in enumerate(order)
        ]
        memory.append((ref, slot, rings))

    def out_tile(j, carry):
        columns = pl.ds(pl.multiple_of(j * 256, 256), 256)
        out_rows[:, columns] = (
            out_w[:, :, :, :, :, :, columns]
            .astype(jnp.float32)
            .reshape(WIDTH, 256)
            .astype(jnp.bfloat16)
        )
        return carry

    lax.fori_loop(0, D // 256, out_tile, 0)

    for ref, slot, rings in memory:
        wires.receive(slot, memory_view(ref, moved(place, "z", 2), 0, WIDTH), across)
        rings[0].open()
    for k in range(2):
        for _, _, rings in memory:
            rings[k].relay()
        for _, _, rings in memory:
            rings[k].close()
            if k == 0:
                rings[1].open()

    query_frame = lax.broadcasted_iota(jnp.int32, (ROWS, ROWS), 0) // SPATIAL
    key_frame = lax.broadcasted_iota(jnp.int32, (ROWS, ROWS), 1) // SPATIAL
    near = (key_frame <= query_frame) & (first_frame + key_frame < limit)
    near_bias = jnp.where(near, 0.0, NEG)
    index = lax.broadcasted_iota(jnp.int32, (1, N_TM * MEM_DEV), 1)
    far = (2 * (index // (SPATIAL // 4)) < limit) & (index // MEM_DEV <= tm)
    far_bias = jnp.where(far, 0.0, NEG)

    def attend(h, carry):
        lanes = pl.ds(pl.multiple_of(h * HD, HD), HD)
        queries = query[:, lanes]
        far_keys = memory_key[:, :, :, :, lanes].reshape(N_TM * MEM_DEV, HD)
        far_values = memory_value[:, :, :, :, lanes].reshape(N_TM * MEM_DEV, HD)
        near_scores = scores_of(queries, key[SPATIAL:, lanes]) * SCALE + near_bias
        far_scores = scores_of(queries, far_keys) * SCALE + far_bias
        top = jnp.maximum(
            jnp.max(near_scores, axis=-1, keepdims=True),
            jnp.max(far_scores, axis=-1, keepdims=True),
        )
        near_weights = jnp.exp2(near_scores - top)
        far_weights = jnp.exp2(far_scores - top)
        total = jnp.sum(near_weights, axis=-1, keepdims=True) + jnp.sum(
            far_weights, axis=-1, keepdims=True
        )
        mixed = weighted(near_weights, value[SPATIAL:, lanes]) + weighted(far_weights, far_values)
        heads[:, lanes] = (mixed / total).astype(jnp.bfloat16)
        return carry

    lax.fori_loop(0, HEADS, attend, 0)

    row_frame = first_frame + lax.broadcasted_iota(jnp.int32, (ROWS, 1), 0) // SPATIAL

    def result_tile(j, carry):
        columns = pl.ds(pl.multiple_of(j * 256, 256), 256)
        result = jnp.dot(heads[...], out_rows[:, columns], preferred_element_type=jnp.float32)
        out[:, columns] = jnp.where(row_frame < limit, result, 0.0).astype(jnp.bfloat16)
        return carry

    lax.fori_loop(0, D // 256, result_tile, 0)
    wires.drain()


N_SLOTS = len(PIECES) * 16 + 1 + 2 * 9


def on_device(
    video,
    norm_gain,
    query_weight,
    key_weight,
    value_weight,
    key_kernel,
    value_kernel,
    out_weight,
    frames_valid,
):
    bf16 = jnp.bfloat16
    gathered = (2, 2, 4, 2, 4)
    vmem = pl.BlockSpec(memory_space=pltpu.VMEM)
    hbm = pl.BlockSpec(memory_space=pl.ANY)
    result = pl.pallas_call(
        body,
        out_shape=jax.ShapeDtypeStruct((ROWS, D), bf16),
        in_specs=[
            hbm,
            vmem,
            hbm,
            hbm,
            hbm,
            vmem,
            vmem,
            hbm,
            pl.BlockSpec(memory_space=pltpu.SMEM),
        ],
        out_specs=vmem,
        scratch_shapes=[
            pltpu.VMEM((EXT, D), bf16),
            pltpu.VMEM((EXT, D), bf16),
            pltpu.VMEM((*gathered, 16, WIDTH), bf16),
            pltpu.VMEM((*gathered, 16, WIDTH), bf16),
            pltpu.VMEM((*gathered, 16, WIDTH), bf16),
            pltpu.VMEM((*gathered, 8, D), bf16),
            pltpu.VMEM((WIDTH, D), bf16),
            pltpu.VMEM((ROWS, WIDTH), bf16),
            pltpu.VMEM((EXT, WIDTH), bf16),
            pltpu.VMEM((EXT, WIDTH), bf16),
            pltpu.VMEM((4, 2, 4, MEM_DEV, WIDTH), bf16),
            pltpu.VMEM((4, 2, 4, MEM_DEV, WIDTH), bf16),
            pltpu.VMEM((HEADS, 2 * MEM_DEV, HD), jnp.float32),
            pltpu.VMEM((HEADS, 2 * MEM_DEV, HD), jnp.float32),
            pltpu.VMEM((ROWS, WIDTH), bf16),
            pltpu.SemaphoreType.DMA((5,)),
            pltpu.SemaphoreType.DMA((N_SLOTS,)),
            pltpu.SemaphoreType.DMA((N_SLOTS,)),
        ],
        compiler_params=pltpu.CompilerParams(
            collective_id=0, has_side_effects=True, vmem_limit_bytes=60 * 1024 * 1024
        ),
        name="memory_attention",
    )(
        video[0],
        norm_gain.reshape(1, D),
        query_weight,
        key_weight,
        value_weight,
        key_kernel,
        value_kernel,
        out_weight,
        frames_valid,
    )
    return result[None]


def solution(mesh):
    in_specs = (
        P("vid", "tm", None),
        P(),
        P(("vid", "tm"), None),
        P(("vid", "tm"), None),
        P(("vid", "tm"), None),
        P(),
        P(),
        P(("vid", "tm"), None),
        P(),
    )
    out_specs = P("vid", "tm", None)
    return jax.shard_map(
        on_device, mesh=mesh, in_specs=in_specs, out_specs=out_specs, check_vma=False
    )
```

```python
import functools
import math

import jax
import jax.numpy as jnp
from jax import lax
from jax.experimental import pallas as pl
from jax.experimental.pallas import tpu as pltpu
from jax.sharding import PartitionSpec as P

MESH = pl.DeviceIdType.MESH
HEADS = 8
HD = 128
SIDE = 8
SPATIAL = SIDE * SIDE
N_TM = 32
ROWS = 256
FRAMES_DEV = ROWS // SPATIAL
EXT = ROWS + SPATIAL
MEM_DEV = 32
D = 2048
WIDTH = HEADS * HD
NEG = -1e30
SCALE = (1.0 / math.sqrt(HD)) * math.log2(math.e)

KEY_VALUE = (
    (1, 0, 768, "xyz"),
    (1, 768, 256, "yzx"),
    (2, 0, 384, "yzx"),
    (2, 384, 640, "zxy"),
)
QUERY = ((0, 0, 384, "xyz"), (0, 384, 384, "yzx"), (0, 768, 256, "zxy"))
OUT = ((3, 0, 1024, "xyz"), (3, 1024, 1024, "yxz"))
PIECES = KEY_VALUE + QUERY + OUT
HALF = WIDTH // 2
MEMORY_ORDERS = ("xy", "yx")
KEYS = ROWS + N_TM * MEM_DEV


def device(place, core):
    x, y, z = place["x"], place["y"], place["z"]
    return (lax.rem(z, 2) * 2 + core, x * 8 + (z // 2) * 4 + y)


def moved(place, axis, steps):
    return {**place, axis: lax.rem(place[axis] + steps + 4, 4)}


def halves(start, size):
    first = (size // 256) * 128 if size > 128 else size
    first = size - first
    return ((start, first), (start + first, size - first))


class Wires:
    def __init__(self, send_sems, recv_sems):
        self.send_sems, self.recv_sems = send_sems, recv_sems
        self.count = 0
        self.started = []

    def slot(self):
        self.count += 1
        return self.count - 1

    def send(self, slot, src, dst, target, start=True):
        copy = pltpu.make_async_remote_copy(
            src_ref=src,
            dst_ref=dst,
            send_sem=self.send_sems.at[slot],
            recv_sem=self.recv_sems.at[slot],
            device_id=target,
            device_id_type=MESH,
        )
        if start:
            copy.start()
        self.started.append(copy)
        return copy

    def receive(self, slot, dst, source):
        pltpu.make_async_remote_copy(
            src_ref=dst,
            dst_ref=dst,
            send_sem=self.send_sems.at[slot],
            recv_sem=self.recv_sems.at[slot],
            device_id=source,
            device_id_type=MESH,
        ).wait_recv()

    def drain(self):
        for copy in self.started:
            copy.wait_send()


def weight_view(ref, core, place, start, size):
    every = slice(None)
    x, y, z = (place[axis] for axis in "xyz")
    zl = every if z is None else lax.rem(z, 2)
    zh = every if z is None else z // 2
    return ref.at[
        zl,
        core,
        every if x is None else x,
        zh,
        every if y is None else y,
        :,
        pl.ds(start, size),
    ]


def memory_view(ref, place, start, size):
    every = slice(None)
    x, y, z = (place[axis] for axis in "xyz")
    return ref.at[
        every if x is None else x,
        every if z is None else z // 2,
        every if y is None else y,
        :,
        pl.ds(start, size),
    ]


class Ring:
    def __init__(self, wires, view, place, core, axis, known, start, size, source=None):
        self.wires, self.place, self.core, self.axis = wires, place, core, axis
        self.source = place if source is None else source
        self.known, self.start, self.size = known, start, size
        self.view = view
        self.slots = [wires.slot() for _ in range(4)]

    def region(self, steps, start, size):
        place = {**moved(self.source, self.axis, steps), **{a: None for a in self.known}}
        return self.view(place, start, size)

    def target(self, steps):
        return device(moved(self.place, self.axis, steps), self.core)

    def open(self, src=None):
        mine = self.region(0, self.start, self.size)
        for slot, steps in zip(self.slots[:2], (1, -1)):
            self.wires.send(slot, mine if src is None else src, mine, self.target(steps))

    def relay(self):
        for slot, steps, part in zip(self.slots[:2], (1, -1), halves(self.start, self.size)):
            self.wires.receive(slot, self.region(-steps, self.start, self.size), self.target(-steps))
        for slot, steps, part in zip(self.slots[2:], (1, -1), halves(self.start, self.size)):
            region = self.region(-steps, *part)
            self.wires.send(slot, region, region, self.target(steps))

    def close(self):
        for slot, steps, part in zip(self.slots[2:], (1, -1), halves(self.start, self.size)):
            self.wires.receive(slot, self.region(2, *part), self.target(-steps))


class Gather:
    def __init__(self, wires, ref, shard, place, core, piece):
        _, self.start, self.size, order = piece
        self.wires, self.ref, self.shard = wires, ref, shard
        self.place, self.core, self.order = place, core, order
        self.partner = device(place, 1 - core)
        self.rings = [
            Ring(
                wires,
                lambda at, start, size: weight_view(ref, core, at, start, size),
                place,
                core,
                axis,
                order[:k],
                self.start,
                self.size,
            )
            for k, axis in enumerate(order)
        ]
        self.slots = [wires.slot() for _ in range(4)]

    def open(self):
        self.rings[0].open(self.shard.at[:, pl.ds(self.start, self.size)])

    def relay(self, k):
        self.rings[k].relay()

    def close(self, k):
        self.rings[k].close()
        if k == 0:
            self.rings[1].open()

    def last(self):
        self.rings[2].open()

    def region(self, core, steps):
        place = {
            **moved(self.place, self.order[2], steps),
            self.order[0]: None,
            self.order[1]: None,
        }
        return weight_view(self.ref, core, place, self.start, self.size)

    def hand(self, k):
        region = self.region(self.core, (0, 1, -1, 2)[k])
        self.wires.send(self.slots[k], region, region, self.partner)

    def take(self):
        for k, steps in enumerate((0, 1, -1, 2)):
            self.wires.receive(self.slots[k], self.region(1 - self.core, steps), self.partner)


def normalize_rows(values, gain):
    center = jnp.mean(values, axis=-1, keepdims=True)
    spread = jnp.mean((values - center) ** 2, axis=-1, keepdims=True)
    return ((values - center) * lax.rsqrt(spread + 1e-06) * gain).astype(jnp.bfloat16)


def project(normed, first, count, weight, core, partial, out):
    def tile(j, carry):
        columns = pl.ds(pl.multiple_of(j * 256, 256), 256)
        total = jnp.zeros((count, 256), jnp.float32) if out is None else partial[:count, columns]
        for zl in range(2):
            rows = weight[zl, core, :, :, :, :, columns].reshape(512, 256)
            depth = pl.ds(pl.multiple_of((zl * 2 + core) * 512, 512), 512)
            total = total + jnp.dot(
                normed[first : first + count, depth], rows, preferred_element_type=jnp.float32
            )
        if out is None:
            partial[:count, columns] = total
        else:
            out[:, columns] = total.astype(jnp.bfloat16)
        return carry

    lax.fori_loop(0, WIDTH // 256, tile, 0)


def pool(source, taps, valid, spread_tmp, out, place):
    column = lax.broadcasted_iota(jnp.int32, (SIDE, HD), 0)

    def head(h, carry):
        lanes = pl.ds(pl.multiple_of(h * HD, HD), HD)
        grid = source[:, lanes].astype(jnp.float32).reshape(FRAMES_DEV + 1, SIDE, SIDE, HD)
        kernel = taps[:, lanes].astype(jnp.float32)
        frames = [jnp.where(valid[f], grid[f], 0.0) for f in range(FRAMES_DEV + 1)]
        for j in range(FRAMES_DEV // 2):
            for a in range(SIDE // 2):
                sums = [jnp.zeros((SIDE, HD), jnp.float32) for _ in range(3)]
                for dt in range(3):
                    for dh in range(3):
                        row = 2 * a + dh - 1
                        if row < 0:
                            continue
                        values = frames[2 * j + 2 - dt][row]
                        for dw in range(3):
                            tap = 9 * dt + 3 * dh + dw
                            sums[dw] = sums[dw] + values * kernel[tap : tap + 1]
                left = jnp.where(column == 0, 0.0, pltpu.roll(sums[0], 1, 0))
                right = pltpu.roll(sums[2], SIDE - 1, 0)
                at = (j * (SIDE // 2) + a) * SIDE
                spread_tmp[h, at : at + SIDE, :] = sums[1] + left + right
        rows = spread_tmp[h, pl.ds(0, MEM_DEV, stride=2), :]
        center = jnp.mean(rows, axis=-1, keepdims=True)
        width = jnp.mean((rows - center) ** 2, axis=-1, keepdims=True)
        normed = (rows - center) * lax.rsqrt(width + 1e-06)
        out[place["x"], place["z"] // 2, place["y"], :, lanes] = normed.astype(jnp.bfloat16)
        return carry

    lax.fori_loop(0, HEADS, head, 0)


def scores_of(queries, keys):
    return lax.dot_general(
        queries, keys, (((1,), (1,)), ((), ())), preferred_element_type=jnp.float32
    )


class Memory:
    def __init__(self, wires, ref, place, core, order, start, own):
        self.rings = [
            Ring(
                wires,
                lambda at, first, size: memory_view(ref, at, first, size),
                place,
                core,
                axis,
                order[:k],
                start,
                HALF,
                place if own else moved(place, "z", 2),
            )
            for k, axis in enumerate(order)
        ]

    def open(self):
        self.rings[0].open()

    def relay(self, k):
        self.rings[k].relay()

    def close(self, k):
        self.rings[k].close()
        if k == 0:
            self.rings[1].open()


def body(
    video,
    gain,
    query_shard,
    key_shard,
    value_shard,
    key_taps,
    value_taps,
    out_shard,
    frames_valid,
    out,
    tokens,
    normed,
    query_w,
    key_w,
    value_w,
    out_w,
    out_rows,
    key_partial,
    value_partial,
    query,
    key,
    value,
    memory_key,
    memory_value,
    spread_key,
    spread_value,
    highs,
    lows,
    totals,
    heads,
    local_sems,
    send_sems,
    recv_sems,
):
    vid, tm = lax.axis_index("vid"), lax.axis_index("tm")
    core = lax.rem(vid, 2)
    place = {
        "x": tm // 8,
        "y": lax.rem(tm, 4),
        "z": lax.rem(tm // 4, 2) * 2 + vid // 2,
    }
    after, before = lax.rem(tm + 1, N_TM), lax.rem(tm + N_TM - 1, N_TM)
    partner = device(place, 1 - core)
    across = device(moved(place, "z", 2), core)

    barrier = pltpu.get_barrier_semaphore()
    greeted = [device(moved(place, axis, steps), core) for axis in "xyz" for steps in (1, -1)]
    greeted.append(partner)
    for other in greeted:
        pl.semaphore_signal(barrier, inc=1, device_id=other, device_id_type=MESH)

    shards = (query_shard, key_shard, value_shard, out_shard)
    weights = (query_w, key_w, value_w, out_w)
    own = [
        pltpu.make_async_copy(
            shard,
            weight.at[vid // 2, core, place["x"], place["z"] // 2, place["y"]],
            local_sems.at[k],
        )
        for k, (shard, weight) in enumerate(zip(shards, weights))
    ]
    own_tokens = pltpu.make_async_copy(video, tokens.at[pl.ds(SPATIAL, ROWS)], local_sems.at[4])
    for copy in own:
        copy.start()
    own_tokens.start()
    pl.semaphore_wait(barrier, len(greeted))

    wires = Wires(send_sems, recv_sems)
    key_value, query_part, out_part = (
        [Gather(wires, weights[p[0]], shards[p[0]], place, core, p) for p in stream]
        for stream in (KEY_VALUE, QUERY, OUT)
    )
    everything = key_value + query_part + out_part
    for gather in everything:
        gather.open()
    halo_slot = wires.slot()
    halo = tokens.at[pl.ds(0, SPATIAL)]

    last_frame = video.at[pl.ds(ROWS - SPATIAL, SPATIAL)]
    halo_copy = wires.send(halo_slot, last_frame, halo, (vid, after), start=False)

    @pl.when(place["y"] < 3)
    def _():
        halo_copy.start()

    for copy in own:
        copy.wait()
    own_tokens.wait()

    scale = gain[...].astype(jnp.float32).reshape(1, D)

    def normalize_at(i, carry):
        at = pl.ds(pl.multiple_of(i * 32, 32), 32)
        normed[at, :] = normalize_rows(tokens[at, :].astype(jnp.float32), scale)
        return carry

    lax.fori_loop(SPATIAL // 32, EXT // 32, normalize_at, 0)
    for k in range(2):
        for gather in everything:
            gather.relay(k)
        for gather in everything:
            gather.close(k)
            if k == 1 and gather in key_value:
                gather.last()

    @pl.when(place["y"] == 3)
    def _():
        halo_copy.start()

    for gather in key_value:
        gather.hand(0)
    for gather in key_value:
        gather.relay(2)
        gather.hand(1)
        gather.hand(2)
    for gather in query_part:
        gather.last()
        gather.hand(0)
    wires.receive(halo_slot, halo, (vid, before))
    lax.fori_loop(0, SPATIAL // 32, normalize_at, 0)
    for gather in key_value:
        gather.close(2)
        gather.hand(3)
    project(normed, 0, EXT, key_w, core, key_partial, None)
    project(normed, 0, EXT, value_w, core, value_partial, None)
    for gather in key_value:
        gather.take()
    for gather in query_part:
        gather.relay(2)
        gather.hand(1)
        gather.hand(2)
    project(normed, 0, EXT, key_w, 1 - core, key_partial, key)
    project(normed, 0, EXT, value_w, 1 - core, value_partial, value)

    limit = frames_valid[vid]
    first_frame = tm * FRAMES_DEV
    valid = [
        (first_frame + f - 1 < limit) & (first_frame + f - 1 >= 0) for f in range(FRAMES_DEV + 1)
    ]
    memories = []
    for source, taps, spread, ref in (
        (key, key_taps, spread_key, memory_key),
        (value, value_taps, spread_value, memory_value),
    ):
        pool(source, taps, valid, spread, ref, place)
        region = memory_view(ref, place, 0, WIDTH)
        slot = wires.slot()
        parts = [
            [
                Memory(wires, ref, place, core, order, number * HALF, own_plane)
                for number, order in enumerate(MEMORY_ORDERS)
            ]
            for own_plane in (True, False)
        ]
        for part in parts[0]:
            part.open()
        wires.send(slot, region, region, across)
        memories.append((ref, slot, parts))
        if ref is memory_key:
            for gather in query_part:
                gather.close(2)
                gather.hand(3)
    for gather in out_part:
        gather.last()
        gather.hand(0)

    for ref, slot, (mine, other) in memories:
        for part in mine:
            part.relay(0)
        wires.receive(slot, memory_view(ref, moved(place, "z", 2), 0, WIDTH), across)
        for part in other:
            part.open()
        for part in mine:
            part.close(0)
    for gather in query_part:
        gather.take()
    project(normed, SPATIAL, ROWS, query_w, core, key_partial, None)
    for _, _, (mine, other) in memories:
        for part in other:
            part.relay(0)
        for part in other:
            part.close(0)
    for _, _, (mine, other) in memories:
        for part in mine:
            part.relay(1)
    for gather in out_part:
        gather.relay(2)
        gather.hand(1)
        gather.hand(2)
    project(normed, SPATIAL, ROWS, query_w, 1 - core, key_partial, query)
    for _, _, (mine, other) in memories:
        for part in other:
            part.relay(1)
    for part in memories[0][2][0] + memories[0][2][1]:
        part.close(1)

    query_frame = lax.broadcasted_iota(jnp.int32, (ROWS, ROWS), 0) // SPATIAL
    key_frame = lax.broadcasted_iota(jnp.int32, (ROWS, ROWS), 1) // SPATIAL
    near = (key_frame <= query_frame) & (first_frame + key_frame < limit)
    near_bias = jnp.where(near, 0.0, NEG)
    index = lax.broadcasted_iota(jnp.int32, (1, N_TM * MEM_DEV), 1)
    far = (2 * (index // (SPATIAL // 4)) < limit) & (index // MEM_DEV <= tm)
    far_bias = jnp.where(far, 0.0, NEG)

    def weigh(h, carry):
        lanes = pl.ds(pl.multiple_of(h * HD, HD), HD)
        queries = query[:, lanes]
        far_keys = memory_key[:, :, :, :, lanes].reshape(N_TM * MEM_DEV, HD)
        near_scores = scores_of(queries, key[SPATIAL:, lanes]) * SCALE + near_bias
        far_scores = scores_of(queries, far_keys) * SCALE + far_bias
        top = jnp.maximum(
            jnp.max(near_scores, axis=-1, keepdims=True),
            jnp.max(far_scores, axis=-1, keepdims=True),
        )
        total = jnp.zeros((ROWS, 1), jnp.float32)
        for first, scores in ((0, near_scores), (ROWS, far_scores)):
            exps = jnp.exp2(scores - top)
            total = total + jnp.sum(exps, axis=-1, keepdims=True)
            high = exps.astype(jnp.bfloat16)
            low = (exps - high.astype(jnp.float32)).astype(jnp.bfloat16)
            highs[h, :, first : first + scores.shape[1]] = high
            lows[h, :, first : first + scores.shape[1]] = low
        totals[h] = jnp.broadcast_to(total, (ROWS, HD))
        return carry

    lax.fori_loop(0, HEADS, weigh, 0)

    for part in memories[1][2][0] + memories[1][2][1]:
        part.close(1)
    for gather in out_part:
        gather.close(2)
        gather.hand(3)

    def mix(h, carry):
        lanes = pl.ds(pl.multiple_of(h * HD, HD), HD)
        near_values = value[SPATIAL:, lanes]
        far_values = memory_value[:, :, :, :, lanes].reshape(N_TM * MEM_DEV, HD)
        mixed = jnp.zeros((ROWS, HD), jnp.float32)
        for part in (highs, lows):
            mixed = mixed + jnp.dot(
                part[h, :, :ROWS], near_values, preferred_element_type=jnp.float32
            )
            mixed = mixed + jnp.dot(
                part[h, :, ROWS:], far_values, preferred_element_type=jnp.float32
            )
        heads[:, lanes] = (mixed / totals[h]).astype(jnp.bfloat16)
        return carry

    lax.fori_loop(0, HEADS, mix, 0)
    for gather in out_part:
        gather.take()

    def out_tile(j, carry):
        columns = pl.ds(pl.multiple_of(j * 256, 256), 256)
        out_rows[:, columns] = (
            out_w[:, :, :, :, :, :, columns]
            .astype(jnp.float32)
            .reshape(WIDTH, 256)
            .astype(jnp.bfloat16)
        )
        return carry

    lax.fori_loop(0, D // 256, out_tile, 0)

    row_frame = first_frame + lax.broadcasted_iota(jnp.int32, (ROWS, 1), 0) // SPATIAL

    def result_tile(j, carry):
        columns = pl.ds(pl.multiple_of(j * 256, 256), 256)
        result = jnp.dot(heads[...], out_rows[:, columns], preferred_element_type=jnp.float32)
        out[:, columns] = jnp.where(row_frame < limit, result, 0.0).astype(jnp.bfloat16)
        return carry

    lax.fori_loop(0, D // 256, result_tile, 0)
    wires.drain()


N_SLOTS = len(PIECES) * 16 + 1 + 2 * (1 + 4 * 8)


def on_device(
    video,
    norm_gain,
    query_weight,
    key_weight,
    value_weight,
    key_kernel,
    value_kernel,
    out_weight,
    frames_valid,
):
    bf16 = jnp.bfloat16
    gathered = (2, 2, 4, 2, 4)
    vmem = pl.BlockSpec(memory_space=pltpu.VMEM)
    hbm = pl.BlockSpec(memory_space=pl.ANY)
    result = pl.pallas_call(
        body,
        out_shape=jax.ShapeDtypeStruct((ROWS, D), bf16),
        in_specs=[
            hbm,
            vmem,
            hbm,
            hbm,
            hbm,
            vmem,
            vmem,
            hbm,
            pl.BlockSpec(memory_space=pltpu.SMEM),
        ],
        out_specs=vmem,
        scratch_shapes=[
            pltpu.VMEM((EXT, D), bf16),
            pltpu.VMEM((EXT, D), bf16),
            pltpu.VMEM((*gathered, 16, WIDTH), bf16),
            pltpu.VMEM((*gathered, 16, WIDTH), bf16),
            pltpu.VMEM((*gathered, 16, WIDTH), bf16),
            pltpu.VMEM((*gathered, 8, D), bf16),
            pltpu.VMEM((WIDTH, D), bf16),
            pltpu.VMEM((EXT, WIDTH), jnp.float32),
            pltpu.VMEM((EXT, WIDTH), jnp.float32),
            pltpu.VMEM((ROWS, WIDTH), bf16),
            pltpu.VMEM((EXT, WIDTH), bf16),
            pltpu.VMEM((EXT, WIDTH), bf16),
            pltpu.VMEM((4, 2, 4, MEM_DEV, WIDTH), bf16),
            pltpu.VMEM((4, 2, 4, MEM_DEV, WIDTH), bf16),
            pltpu.VMEM((HEADS, 2 * MEM_DEV, HD), jnp.float32),
            pltpu.VMEM((HEADS, 2 * MEM_DEV, HD), jnp.float32),
            pltpu.VMEM((HEADS, ROWS, KEYS), bf16),
            pltpu.VMEM((HEADS, ROWS, KEYS), bf16),
            pltpu.VMEM((HEADS, ROWS, HD), jnp.float32),
            pltpu.VMEM((ROWS, WIDTH), bf16),
            pltpu.SemaphoreType.DMA((5,)),
            pltpu.SemaphoreType.DMA((N_SLOTS,)),
            pltpu.SemaphoreType.DMA((N_SLOTS,)),
        ],
        compiler_params=pltpu.CompilerParams(
            collective_id=0, has_side_effects=True, vmem_limit_bytes=60 * 1024 * 1024
        ),
        name="memory_attention",
    )(
        video[0],
        norm_gain,
        query_weight,
        key_weight,
        value_weight,
        key_kernel,
        value_kernel,
        out_weight,
        frames_valid,
    )
    return result[None]


def solution(mesh):
    in_specs = (
        P("vid", "tm", None),
        P(),
        P(("vid", "tm"), None),
        P(("vid", "tm"), None),
        P(("vid", "tm"), None),
        P(),
        P(),
        P(("vid", "tm"), None),
        P(),
    )
    out_specs = P("vid", "tm", None)
    return jax.shard_map(
        on_device, mesh=mesh, in_specs=in_specs, out_specs=out_specs, check_vma=False
    )
```

```python
import functools
import math

import jax
import jax.numpy as jnp
from jax import lax
from jax.experimental import pallas as pl
from jax.experimental.pallas import tpu as pltpu
from jax.sharding import PartitionSpec as P

MESH = pl.DeviceIdType.MESH
HEADS = 8
HD = 128
SIDE = 8
SPATIAL = SIDE * SIDE
N_TM = 32
ROWS = 256
FRAMES_DEV = ROWS // SPATIAL
EXT = ROWS + SPATIAL
MEM_DEV = 32
D = 2048
WIDTH = HEADS * HD
NEG = -1e30
SCALE = (1.0 / math.sqrt(HD)) * math.log2(math.e)

KEY_VALUE = (
    (1, 0, 768, "xyz"),
    (1, 768, 256, "yzx"),
    (2, 0, 384, "yzx"),
    (2, 384, 640, "zxy"),
)
QUERY = ((0, 0, 384, "xyz"), (0, 384, 384, "yzx"), (0, 768, 256, "zxy"))
OUT = ((3, 0, 1024, "xyz"), (3, 1024, 1024, "yxz"))
PIECES = KEY_VALUE + QUERY + OUT
HALF = WIDTH // 2
MEMORY_ORDERS = ("xy", "yx")
KEYS = ROWS + N_TM * MEM_DEV


def device(place, core):
    x, y, z = place["x"], place["y"], place["z"]
    return (lax.rem(z, 2) * 2 + core, x * 8 + (z // 2) * 4 + y)


def moved(place, axis, steps):
    return {**place, axis: lax.rem(place[axis] + steps + 4, 4)}


def halves(start, size):
    first = (size // 256) * 128 if size > 128 else size
    first = size - first
    return ((start, first), (start + first, size - first))


class Wires:
    def __init__(self, send_sems, recv_sems):
        self.send_sems, self.recv_sems = send_sems, recv_sems
        self.count = 0
        self.started = []

    def slot(self):
        self.count += 1
        return self.count - 1

    def send(self, slot, src, dst, target, start=True):
        copy = pltpu.make_async_remote_copy(
            src_ref=src,
            dst_ref=dst,
            send_sem=self.send_sems.at[slot],
            recv_sem=self.recv_sems.at[slot],
            device_id=target,
            device_id_type=MESH,
        )
        if start:
            copy.start()
        self.started.append(copy)
        return copy

    def receive(self, slot, dst, source):
        pltpu.make_async_remote_copy(
            src_ref=dst,
            dst_ref=dst,
            send_sem=self.send_sems.at[slot],
            recv_sem=self.recv_sems.at[slot],
            device_id=source,
            device_id_type=MESH,
        ).wait_recv()

    def drain(self):
        for copy in self.started:
            copy.wait_send()


def weight_view(ref, core, place, start, size):
    every = slice(None)
    x, y, z = (place[axis] for axis in "xyz")
    zl = every if z is None else lax.rem(z, 2)
    zh = every if z is None else z // 2
    return ref.at[
        zl,
        core,
        every if x is None else x,
        zh,
        every if y is None else y,
        :,
        pl.ds(start, size),
    ]


def memory_view(ref, place, start, size):
    every = slice(None)
    x, y, z = (place[axis] for axis in "xyz")
    return ref.at[
        every if x is None else x,
        every if z is None else z // 2,
        every if y is None else y,
        :,
        pl.ds(start, size),
    ]


class Phase:
    def __init__(self, wires, view, place, core, axis, known, start, size, source=None):
        self.wires, self.view, self.place, self.core = wires, view, place, core
        self.axis, self.known, self.start, self.size = axis, known, start, size
        self.source = place if source is None else source
        self.slots = [wires.slot() for _ in range(self.count)]

    def region(self, steps, start, size):
        place = {**moved(self.source, self.axis, steps), **{a: None for a in self.known}}
        return self.view(place, start, size)

    def target(self, steps):
        return device(moved(self.place, self.axis, steps), self.core)

    def send(self, number, steps, part, src=None, of=0):
        region = self.region(of, *part)
        src = region if src is None else src
        self.wires.send(self.slots[number], src, region, self.target(steps))

    def receive(self, number, steps, part, of):
        self.wires.receive(self.slots[number], self.region(of, *part), self.target(-steps))


class Direct(Phase):
    count = 3

    def open(self, src=None):
        for number, steps in enumerate((1, -1, 2)):
            self.send(number, steps, (self.start, self.size), src)

    def take(self, number):
        steps = (1, -1, 2)[number]
        self.receive(number, steps, (self.start, self.size), -steps)

    def close(self):
        for number in range(3):
            self.take(number)


class Ring(Phase):
    count = 4

    def open(self):
        for number, steps in enumerate((1, -1)):
            self.send(number, steps, (self.start, self.size))

    def relay(self):
        parts = halves(self.start, self.size)
        for number, steps in enumerate((1, -1)):
            self.receive(number, steps, (self.start, self.size), -steps)
            self.send(number + 2, steps, parts[number], of=-steps)

    def close(self):
        parts = halves(self.start, self.size)
        for number, steps in enumerate((1, -1)):
            self.receive(number + 2, steps, parts[number], 2)


class Gather:
    def __init__(self, wires, ref, shard, place, core, piece):
        _, self.start, self.size, order = piece
        self.wires, self.ref, self.shard = wires, ref, shard
        self.place, self.core, self.order = place, core, order
        self.partner = device(place, 1 - core)
        common = (
            wires,
            lambda at, start, size: weight_view(ref, core, at, start, size),
            place,
            core,
        )
        first, second, third = order
        self.first = Direct(*common, first, "", self.start, self.size)
        self.second = Direct(*common, second, first, self.start, self.size)
        self.rows = [
            Ring(*common, third, first, self.start, self.size, moved(place, second, steps))
            for steps in (0, -1, 1, 2)
        ]
        self.slots = [wires.slot() for _ in range(4)]

    def open(self):
        self.first.open(self.shard.at[:, pl.ds(self.start, self.size)])

    def spread(self, on=True):
        self.first.close()
        self.second.open()
        if on:
            self.rows[0].open()

    def rise(self, on=True):
        for number in range(3):
            self.second.take(number)
            if on:
                self.rows[number + 1].open()

    def last(self):
        for row in self.rows:
            row.open()

    def relay(self):
        for row in self.rows:
            row.relay()

    def close(self):
        for row in self.rows:
            row.close()

    def region(self, core, steps):
        place = {
            **moved(self.place, self.order[2], steps),
            self.order[0]: None,
            self.order[1]: None,
        }
        return weight_view(self.ref, core, place, self.start, self.size)

    def hand(self, k):
        region = self.region(self.core, (0, 1, -1, 2)[k])
        self.wires.send(self.slots[k], region, region, self.partner)

    def take(self):
        for k, steps in enumerate((0, 1, -1, 2)):
            self.wires.receive(self.slots[k], self.region(1 - self.core, steps), self.partner)


def normalize_rows(values, gain):
    center = jnp.mean(values, axis=-1, keepdims=True)
    spread = jnp.mean((values - center) ** 2, axis=-1, keepdims=True)
    return ((values - center) * lax.rsqrt(spread + 1e-06) * gain).astype(jnp.bfloat16)


def project(normed, first, count, weight, core, partial, out):
    def tile(j, carry):
        columns = pl.ds(pl.multiple_of(j * 256, 256), 256)
        total = jnp.zeros((count, 256), jnp.float32) if out is None else partial[:count, columns]
        for zl in range(2):
            rows = weight[zl, core, :, :, :, :, columns].reshape(512, 256)
            depth = pl.ds(pl.multiple_of((zl * 2 + core) * 512, 512), 512)
            total = total + jnp.dot(
                normed[first : first + count, depth], rows, preferred_element_type=jnp.float32
            )
        if out is None:
            partial[:count, columns] = total
        else:
            out[:, columns] = total.astype(jnp.bfloat16)
        return carry

    lax.fori_loop(0, WIDTH // 256, tile, 0)


def pool(source, taps, valid, spread_tmp, out, place):
    column = lax.broadcasted_iota(jnp.int32, (SIDE, HD), 0)

    def head(h, carry):
        lanes = pl.ds(pl.multiple_of(h * HD, HD), HD)
        grid = source[:, lanes].astype(jnp.float32).reshape(FRAMES_DEV + 1, SIDE, SIDE, HD)
        kernel = taps[:, lanes].astype(jnp.float32)
        frames = [jnp.where(valid[f], grid[f], 0.0) for f in range(FRAMES_DEV + 1)]
        for j in range(FRAMES_DEV // 2):
            for a in range(SIDE // 2):
                sums = [jnp.zeros((SIDE, HD), jnp.float32) for _ in range(3)]
                for dt in range(3):
                    for dh in range(3):
                        row = 2 * a + dh - 1
                        if row < 0:
                            continue
                        values = frames[2 * j + 2 - dt][row]
                        for dw in range(3):
                            tap = 9 * dt + 3 * dh + dw
                            sums[dw] = sums[dw] + values * kernel[tap : tap + 1]
                left = jnp.where(column == 0, 0.0, pltpu.roll(sums[0], 1, 0))
                right = pltpu.roll(sums[2], SIDE - 1, 0)
                at = (j * (SIDE // 2) + a) * SIDE
                spread_tmp[h, at : at + SIDE, :] = sums[1] + left + right
        rows = spread_tmp[h, pl.ds(0, MEM_DEV, stride=2), :]
        center = jnp.mean(rows, axis=-1, keepdims=True)
        width = jnp.mean((rows - center) ** 2, axis=-1, keepdims=True)
        normed = (rows - center) * lax.rsqrt(width + 1e-06)
        out[place["x"], place["z"] // 2, place["y"], :, lanes] = normed.astype(jnp.bfloat16)
        return carry

    lax.fori_loop(0, HEADS, head, 0)


def scores_of(queries, keys):
    return lax.dot_general(
        queries, keys, (((1,), (1,)), ((), ())), preferred_element_type=jnp.float32
    )


class Memory:
    def __init__(self, wires, ref, place, core, order, start, own):
        common = (
            wires,
            lambda at, first, size: memory_view(ref, at, first, size),
            place,
            core,
        )
        source = place if own else moved(place, "z", 2)
        self.first = Direct(*common, order[0], "", start, HALF, source)
        self.second = Ring(*common, order[1], order[0], start, HALF, source)


def body(
    video,
    gain,
    query_shard,
    key_shard,
    value_shard,
    key_taps,
    value_taps,
    out_shard,
    frames_valid,
    out,
    tokens,
    normed,
    query_w,
    key_w,
    value_w,
    out_w,
    out_rows,
    key_partial,
    value_partial,
    query,
    key,
    value,
    memory_key,
    memory_value,
    spread_key,
    spread_value,
    shares,
    totals,
    heads,
    local_sems,
    send_sems,
    recv_sems,
):
    vid, tm = lax.axis_index("vid"), lax.axis_index("tm")
    core = lax.rem(vid, 2)
    place = {
        "x": tm // 8,
        "y": lax.rem(tm, 4),
        "z": lax.rem(tm // 4, 2) * 2 + vid // 2,
    }
    after, before = lax.rem(tm + 1, N_TM), lax.rem(tm + N_TM - 1, N_TM)
    partner = device(place, 1 - core)
    across = device(moved(place, "z", 2), core)

    barrier = pltpu.get_barrier_semaphore()
    greeted = [device(moved(place, axis, steps), core) for axis in "xyz" for steps in (1, -1)]
    greeted += [device(moved(place, axis, 2), core) for axis in "xyz"]
    greeted.append(partner)
    greeted.append(device(moved(moved(place, "x", -1), "y", -1), core))
    for other in greeted:
        pl.semaphore_signal(barrier, inc=1, device_id=other, device_id_type=MESH)

    shards = (query_shard, key_shard, value_shard, out_shard)
    weights = (query_w, key_w, value_w, out_w)
    own = [
        pltpu.make_async_copy(
            shard,
            weight.at[vid // 2, core, place["x"], place["z"] // 2, place["y"]],
            local_sems.at[k],
        )
        for k, (shard, weight) in enumerate(zip(shards, weights))
    ]
    own_tokens = pltpu.make_async_copy(video, tokens.at[pl.ds(SPATIAL, ROWS)], local_sems.at[4])
    for copy in own:
        copy.start()
    own_tokens.start()
    pl.semaphore_wait(barrier, len(greeted))

    wires = Wires(send_sems, recv_sems)
    key_value, query_part, out_part = (
        [Gather(wires, weights[p[0]], shards[p[0]], place, core, p) for p in stream]
        for stream in (KEY_VALUE, QUERY, OUT)
    )
    everything = key_value + query_part + out_part
    for gather in everything:
        gather.open()
    halo_slot = wires.slot()
    halo = tokens.at[pl.ds(0, SPATIAL)]

    last_frame = video.at[pl.ds(ROWS - SPATIAL, SPATIAL)]
    halo_copy = wires.send(halo_slot, last_frame, halo, (vid, after), start=False)

    @pl.when(place["y"] < 3)
    def _():
        halo_copy.start()

    for copy in own:
        copy.wait()
    own_tokens.wait()

    scale = gain[...].astype(jnp.float32).reshape(1, D)

    def normalize_at(i, carry):
        at = pl.ds(pl.multiple_of(i * 32, 32), 32)
        normed[at, :] = normalize_rows(tokens[at, :].astype(jnp.float32), scale)
        return carry

    lax.fori_loop(SPATIAL // 32, EXT // 32, normalize_at, 0)
    for gather in key_value:
        gather.spread()

    @pl.when(place["y"] == 3)
    def _():
        halo_copy.start()

    for gather in key_value:
        gather.rise()
        gather.hand(0)

    for number in range(4):
        for gather in key_value:
            gather.rows[number].relay()
    for gather in query_part:
        gather.spread()
    for gather in out_part:
        gather.spread(False)
    for gather in key_value:
        gather.hand(1)
        gather.hand(2)
    for gather in key_value:
        gather.close()
        gather.hand(3)
    for gather in query_part:
        gather.rise()
        gather.hand(0)
    wires.receive(halo_slot, halo, (vid, before))
    lax.fori_loop(0, SPATIAL // 32, normalize_at, 0)
    project(normed, 0, EXT, key_w, core, key_partial, None)
    project(normed, 0, EXT, value_w, core, value_partial, None)
    for gather in key_value:
        gather.take()
    for gather in query_part:
        gather.relay()
        gather.hand(1)
        gather.hand(2)
    project(normed, 0, EXT, key_w, 1 - core, key_partial, key)
    project(normed, 0, EXT, value_w, 1 - core, value_partial, value)

    limit = frames_valid[vid]
    first_frame = tm * FRAMES_DEV
    valid = [
        (first_frame + f - 1 < limit) & (first_frame + f - 1 >= 0) for f in range(FRAMES_DEV + 1)
    ]
    memories = []
    for source, taps, spread, ref in (
        (key, key_taps, spread_key, memory_key),
        (value, value_taps, spread_value, memory_value),
    ):
        pool(source, taps, valid, spread, ref, place)
        region = memory_view(ref, place, 0, WIDTH)
        slot = wires.slot()
        mine, other = (
            [
                Memory(wires, ref, place, core, order, number * HALF, own_plane)
                for number, order in enumerate(MEMORY_ORDERS)
            ]
            for own_plane in (True, False)
        )
        wires.send(slot, region, region, across)
        for part in mine:
            part.first.open()
        memories.append((ref, slot, mine, other))
        if ref is memory_key:
            for gather in query_part:
                gather.close()
                gather.hand(3)
    for gather in out_part:
        gather.rise(False)
        gather.last()
        gather.hand(0)

    (key_ref, key_slot, key_mine, key_other), (value_ref, value_slot, value_mine, value_other) = memories
    far_place = moved(place, "z", 2)
    for part in key_mine:
        part.first.close()
        part.second.open()
    wires.receive(key_slot, memory_view(key_ref, far_place, 0, WIDTH), across)
    for part in key_other:
        part.first.open()
    for part in value_mine:
        part.first.close()
    wires.receive(value_slot, memory_view(value_ref, far_place, 0, WIDTH), across)
    for part in value_other:
        part.first.open()
    for part in key_other:
        part.first.close()
        part.second.open()
    for part in value_mine:
        part.second.open()
    for part in key_mine:
        part.second.relay()
    for gather in query_part:
        gather.take()
    project(normed, SPATIAL, ROWS, query_w, core, key_partial, None)
    for part in value_other:
        part.first.close()
        part.second.open()
    for part in key_other:
        part.second.relay()
    project(normed, SPATIAL, ROWS, query_w, 1 - core, key_partial, query)
    for part in value_mine:
        part.second.relay()
    for gather in out_part:
        gather.relay()
        gather.hand(1)
        gather.hand(2)
    for part in key_mine + key_other:
        part.second.close()

    query_frame = lax.broadcasted_iota(jnp.int32, (ROWS, ROWS), 0) // SPATIAL
    key_frame = lax.broadcasted_iota(jnp.int32, (ROWS, ROWS), 1) // SPATIAL
    near = (key_frame <= query_frame) & (first_frame + key_frame < limit)
    near_bias = jnp.where(near, 0.0, NEG)
    index = lax.broadcasted_iota(jnp.int32, (1, N_TM * MEM_DEV), 1)
    far = (2 * (index // (SPATIAL // 4)) < limit) & (index // MEM_DEV <= tm)
    far_bias = jnp.where(far, 0.0, NEG)

    def weigh(h, carry):
        lanes = pl.ds(pl.multiple_of(h * HD, HD), HD)
        queries = query[:, lanes]
        far_keys = memory_key[:, :, :, :, lanes].reshape(N_TM * MEM_DEV, HD)
        near_scores = scores_of(queries, key[SPATIAL:, lanes]) * SCALE + near_bias
        far_scores = scores_of(queries, far_keys) * SCALE + far_bias
        top = jnp.maximum(
            jnp.max(near_scores, axis=-1, keepdims=True),
            jnp.max(far_scores, axis=-1, keepdims=True),
        )
        total = jnp.zeros((ROWS, 1), jnp.float32)
        for first, scores in ((0, near_scores), (ROWS, far_scores)):
            exps = jnp.exp2(scores - top)
            total = total + jnp.sum(exps, axis=-1, keepdims=True)
            shares[h, :, first : first + scores.shape[1]] = exps.astype(jnp.bfloat16)
        totals[h] = jnp.broadcast_to(total, (ROWS, HD))
        return carry

    lax.fori_loop(0, HEADS // 2, weigh, 0)
    for part in value_other:
        part.second.relay()
    lax.fori_loop(HEADS // 2, HEADS, weigh, 0)

    for gather in out_part:
        gather.close()
        gather.hand(3)
    for gather in out_part:
        gather.take()

    def out_tile(j, carry):
        columns = pl.ds(pl.multiple_of(j * 256, 256), 256)
        out_rows[:, columns] = (
            out_w[:, :, :, :, :, :, columns]
            .astype(jnp.float32)
            .reshape(WIDTH, 256)
            .astype(jnp.bfloat16)
        )
        return carry

    lax.fori_loop(0, D // 256, out_tile, 0)

    for part in value_mine + value_other:
        part.second.close()

    def mix(h, carry):
        lanes = pl.ds(pl.multiple_of(h * HD, HD), HD)
        near_values = value[SPATIAL:, lanes]
        far_values = memory_value[:, :, :, :, lanes].reshape(N_TM * MEM_DEV, HD)
        mixed = jnp.dot(shares[h, :, :ROWS], near_values, preferred_element_type=jnp.float32)
        mixed = mixed + jnp.dot(
            shares[h, :, ROWS:], far_values, preferred_element_type=jnp.float32
        )
        heads[:, lanes] = (mixed / totals[h]).astype(jnp.bfloat16)
        return carry

    lax.fori_loop(0, HEADS, mix, 0)
    row_frame = first_frame + lax.broadcasted_iota(jnp.int32, (ROWS, 1), 0) // SPATIAL

    def result_tile(j, carry):
        columns = pl.ds(pl.multiple_of(j * 256, 256), 256)
        result = jnp.dot(heads[...], out_rows[:, columns], preferred_element_type=jnp.float32)
        out[:, columns] = jnp.where(row_frame < limit, result, 0.0).astype(jnp.bfloat16)
        return carry

    lax.fori_loop(0, D // 256, result_tile, 0)
    wires.drain()


N_SLOTS = len(PIECES) * 26 + 1 + 2 * (1 + 4 * 7)


def on_device(
    video,
    norm_gain,
    query_weight,
    key_weight,
    value_weight,
    key_kernel,
    value_kernel,
    out_weight,
    frames_valid,
):
    bf16 = jnp.bfloat16
    gathered = (2, 2, 4, 2, 4)
    vmem = pl.BlockSpec(memory_space=pltpu.VMEM)
    hbm = pl.BlockSpec(memory_space=pl.ANY)
    result = pl.pallas_call(
        body,
        out_shape=jax.ShapeDtypeStruct((ROWS, D), bf16),
        in_specs=[
            hbm,
            vmem,
            hbm,
            hbm,
            hbm,
            vmem,
            vmem,
            hbm,
            pl.BlockSpec(memory_space=pltpu.SMEM),
        ],
        out_specs=vmem,
        scratch_shapes=[
            pltpu.VMEM((EXT, D), bf16),
            pltpu.VMEM((EXT, D), bf16),
            pltpu.VMEM((*gathered, 16, WIDTH), bf16),
            pltpu.VMEM((*gathered, 16, WIDTH), bf16),
            pltpu.VMEM((*gathered, 16, WIDTH), bf16),
            pltpu.VMEM((*gathered, 8, D), bf16),
            pltpu.VMEM((WIDTH, D), bf16),
            pltpu.VMEM((EXT, WIDTH), jnp.float32),
            pltpu.VMEM((EXT, WIDTH), jnp.float32),
            pltpu.VMEM((ROWS, WIDTH), bf16),
            pltpu.VMEM((EXT, WIDTH), bf16),
            pltpu.VMEM((EXT, WIDTH), bf16),
            pltpu.VMEM((4, 2, 4, MEM_DEV, WIDTH), bf16),
            pltpu.VMEM((4, 2, 4, MEM_DEV, WIDTH), bf16),
            pltpu.VMEM((HEADS, 2 * MEM_DEV, HD), jnp.float32),
            pltpu.VMEM((HEADS, 2 * MEM_DEV, HD), jnp.float32),
            pltpu.VMEM((HEADS, ROWS, KEYS), bf16),
            pltpu.VMEM((HEADS, ROWS, HD), jnp.float32),
            pltpu.VMEM((ROWS, WIDTH), bf16),
            pltpu.SemaphoreType.DMA((5,)),
            pltpu.SemaphoreType.DMA((N_SLOTS,)),
            pltpu.SemaphoreType.DMA((N_SLOTS,)),
        ],
        compiler_params=pltpu.CompilerParams(
            collective_id=0, has_side_effects=True, vmem_limit_bytes=60 * 1024 * 1024
        ),
        name="memory_attention",
    )(
        video[0],
        norm_gain,
        query_weight,
        key_weight,
        value_weight,
        key_kernel,
        value_kernel,
        out_weight,
        frames_valid,
    )
    return result[None]


def solution(mesh):
    in_specs = (
        P("vid", "tm", None),
        P(),
        P(("vid", "tm"), None),
        P(("vid", "tm"), None),
        P(("vid", "tm"), None),
        P(),
        P(),
        P(("vid", "tm"), None),
        P(),
    )
    out_specs = P("vid", "tm", None)
    return jax.shard_map(
        on_device, mesh=mesh, in_specs=in_specs, out_specs=out_specs, check_vma=False
    )
```

```python
import functools
import math

import jax
import jax.numpy as jnp
from jax import lax
from jax.experimental import pallas as pl
from jax.experimental.pallas import tpu as pltpu
from jax.sharding import PartitionSpec as P

MESH = pl.DeviceIdType.MESH
HEADS = 8
HD = 128
SIDE = 8
SPATIAL = SIDE * SIDE
N_TM = 32
ROWS = 256
FRAMES_DEV = ROWS // SPATIAL
EXT = ROWS + SPATIAL
MEM_DEV = 32
D = 2048
WIDTH = HEADS * HD
NEG = -1e30
SCALE = (1.0 / math.sqrt(HD)) * math.log2(math.e)

KEY_VALUE = (
    (1, 0, 768, "xyz"),
    (1, 768, 256, "yzx"),
    (2, 0, 384, "yzx"),
    (2, 384, 640, "zxy"),
)
QUERY = ((0, 0, 384, "xyz"), (0, 384, 384, "yzx"), (0, 768, 256, "zxy"))
OUT = ((3, 0, 1024, "xyz"), (3, 1024, 1024, "yxz"))
PIECES = KEY_VALUE + QUERY + OUT
HALF = WIDTH // 2
MEMORY_ORDERS = ("xy", "yx")
KEYS = ROWS + N_TM * MEM_DEV


def device(place, core):
    x, y, z = place["x"], place["y"], place["z"]
    return (lax.rem(z, 2) * 2 + core, x * 8 + (z // 2) * 4 + y)


def moved(place, axis, steps):
    return {**place, axis: lax.rem(place[axis] + steps + 4, 4)}


def halves(start, size):
    first = (size // 256) * 128 if size > 128 else size
    first = size - first
    return ((start, first), (start + first, size - first))


class Wires:
    def __init__(self, send_sems, recv_sems):
        self.send_sems, self.recv_sems = send_sems, recv_sems
        self.count = 0
        self.started = []

    def slot(self):
        self.count += 1
        return self.count - 1

    def send(self, slot, src, dst, target, start=True):
        copy = pltpu.make_async_remote_copy(
            src_ref=src,
            dst_ref=dst,
            send_sem=self.send_sems.at[slot],
            recv_sem=self.recv_sems.at[slot],
            device_id=target,
            device_id_type=MESH,
        )
        if start:
            copy.start()
        self.started.append(copy)
        return copy

    def receive(self, slot, dst, source):
        pltpu.make_async_remote_copy(
            src_ref=dst,
            dst_ref=dst,
            send_sem=self.send_sems.at[slot],
            recv_sem=self.recv_sems.at[slot],
            device_id=source,
            device_id_type=MESH,
        ).wait_recv()

    def drain(self):
        for copy in self.started:
            copy.wait_send()


def weight_view(ref, core, place, start, size):
    every = slice(None)
    x, y, z = (place[axis] for axis in "xyz")
    zl = every if z is None else lax.rem(z, 2)
    zh = every if z is None else z // 2
    return ref.at[
        zl,
        core,
        every if x is None else x,
        zh,
        every if y is None else y,
        :,
        pl.ds(start, size),
    ]


def memory_view(ref, place, start, size):
    every = slice(None)
    x, y, z = (place[axis] for axis in "xyz")
    return ref.at[
        every if x is None else x,
        every if z is None else z // 2,
        every if y is None else y,
        :,
        pl.ds(start, size),
    ]


class Phase:
    def __init__(self, wires, view, place, core, axis, known, start, size, source=None):
        self.wires, self.view, self.place, self.core = wires, view, place, core
        self.axis, self.known, self.start, self.size = axis, known, start, size
        self.source = place if source is None else source
        self.slots = [wires.slot() for _ in range(self.count)]

    def region(self, steps, start, size):
        place = {**moved(self.source, self.axis, steps), **{a: None for a in self.known}}
        return self.view(place, start, size)

    def target(self, steps):
        return device(moved(self.place, self.axis, steps), self.core)

    def send(self, number, steps, part, src=None, of=0):
        region = self.region(of, *part)
        src = region if src is None else src
        self.wires.send(self.slots[number], src, region, self.target(steps))

    def receive(self, number, steps, part, of):
        self.wires.receive(self.slots[number], self.region(of, *part), self.target(-steps))


class Direct(Phase):
    count = 3

    def open(self, src=None):
        for number, steps in enumerate((1, -1, 2)):
            self.send(number, steps, (self.start, self.size), src)

    def take(self, number):
        steps = (1, -1, 2)[number]
        self.receive(number, steps, (self.start, self.size), -steps)

    def close(self):
        for number in range(3):
            self.take(number)


class Ring(Phase):
    count = 4

    def open(self):
        for number, steps in enumerate((1, -1)):
            self.send(number, steps, (self.start, self.size))

    def relay(self):
        parts = halves(self.start, self.size)
        for number, steps in enumerate((1, -1)):
            self.receive(number, steps, (self.start, self.size), -steps)
            self.send(number + 2, steps, parts[number], of=-steps)

    def close(self):
        parts = halves(self.start, self.size)
        for number, steps in enumerate((1, -1)):
            self.receive(number + 2, steps, parts[number], 2)


class Gather:
    def __init__(self, wires, ref, shard, place, core, piece):
        _, self.start, self.size, order = piece
        self.wires, self.ref, self.shard = wires, ref, shard
        self.place, self.core, self.order = place, core, order
        self.partner = device(place, 1 - core)
        common = (
            wires,
            lambda at, start, size: weight_view(ref, core, at, start, size),
            place,
            core,
        )
        first, second, third = order
        self.first = Direct(*common, first, "", self.start, self.size)
        self.second = Direct(*common, second, first, self.start, self.size)
        self.rows = [
            Ring(*common, third, first, self.start, self.size, moved(place, second, steps))
            for steps in (0, -1, 1, 2)
        ]
        self.slots = [wires.slot() for _ in range(4)]

    def open(self):
        self.first.open(self.shard.at[:, pl.ds(self.start, self.size)])

    def spread(self, on=True):
        self.first.close()
        self.second.open()
        if on:
            self.rows[0].open()

    def rise(self, on=True):
        for number in range(3):
            self.second.take(number)
            if on:
                self.rows[number + 1].open()

    def last(self):
        for row in self.rows:
            row.open()

    def relay(self):
        for row in self.rows:
            row.relay()

    def close(self):
        for row in self.rows:
            row.close()

    def region(self, core, steps):
        place = {
            **moved(self.place, self.order[2], steps),
            self.order[0]: None,
            self.order[1]: None,
        }
        return weight_view(self.ref, core, place, self.start, self.size)

    def hand(self, k):
        region = self.region(self.core, (0, 1, -1, 2)[k])
        self.wires.send(self.slots[k], region, region, self.partner)

    def take(self):
        for k, steps in enumerate((0, 1, -1, 2)):
            self.wires.receive(self.slots[k], self.region(1 - self.core, steps), self.partner)


def normalize_rows(values, gain):
    center = jnp.mean(values, axis=-1, keepdims=True)
    spread = jnp.mean((values - center) ** 2, axis=-1, keepdims=True)
    return ((values - center) * lax.rsqrt(spread + 1e-06) * gain).astype(jnp.bfloat16)


def project(normed, first, count, weight, core, partial, out):
    def tile(j, carry):
        columns = pl.ds(pl.multiple_of(j * 256, 256), 256)
        total = jnp.zeros((count, 256), jnp.float32) if out is None else partial[:count, columns]
        for zl in range(2):
            rows = weight[zl, core, :, :, :, :, columns].reshape(512, 256)
            depth = pl.ds(pl.multiple_of((zl * 2 + core) * 512, 512), 512)
            total = total + jnp.dot(
                normed[first : first + count, depth], rows, preferred_element_type=jnp.float32
            )
        if out is None:
            partial[:count, columns] = total
        else:
            out[:, columns] = total.astype(jnp.bfloat16)
        return carry

    lax.fori_loop(0, WIDTH // 256, tile, 0)


def pool(source, taps, valid, spread_tmp, out, place):
    column = lax.broadcasted_iota(jnp.int32, (SIDE, HD), 0)

    def head(h, carry):
        lanes = pl.ds(pl.multiple_of(h * HD, HD), HD)
        grid = source[:, lanes].astype(jnp.float32).reshape(FRAMES_DEV + 1, SIDE, SIDE, HD)
        kernel = taps[:, lanes].astype(jnp.float32)
        frames = [jnp.where(valid[f], grid[f], 0.0) for f in range(FRAMES_DEV + 1)]
        for j in range(FRAMES_DEV // 2):
            for a in range(SIDE // 2):
                sums = [jnp.zeros((SIDE, HD), jnp.float32) for _ in range(3)]
                for dt in range(3):
                    for dh in range(3):
                        row = 2 * a + dh - 1
                        if row < 0:
                            continue
                        values = frames[2 * j + 2 - dt][row]
                        for dw in range(3):
                            tap = 9 * dt + 3 * dh + dw
                            sums[dw] = sums[dw] + values * kernel[tap : tap + 1]
                left = jnp.where(column == 0, 0.0, pltpu.roll(sums[0], 1, 0))
                right = pltpu.roll(sums[2], SIDE - 1, 0)
                at = (j * (SIDE // 2) + a) * SIDE
                spread_tmp[h, at : at + SIDE, :] = sums[1] + left + right
        rows = spread_tmp[h, pl.ds(0, MEM_DEV, stride=2), :]
        center = jnp.mean(rows, axis=-1, keepdims=True)
        width = jnp.mean((rows - center) ** 2, axis=-1, keepdims=True)
        normed = (rows - center) * lax.rsqrt(width + 1e-06)
        out[place["x"], place["z"] // 2, place["y"], :, lanes] = normed.astype(jnp.bfloat16)
        return carry

    lax.fori_loop(0, HEADS, head, 0)


def scores_of(queries, keys):
    return lax.dot_general(
        queries, keys, (((1,), (1,)), ((), ())), preferred_element_type=jnp.float32
    )


class Memory:
    def __init__(self, wires, ref, place, core, order, start, own):
        common = (
            wires,
            lambda at, first, size: memory_view(ref, at, first, size),
            place,
            core,
        )
        source = place if own else moved(place, "z", 2)
        self.first = Direct(*common, order[0], "", start, HALF, source)
        self.second = Ring(*common, order[1], order[0], start, HALF, source)


def body(
    video,
    gain,
    query_shard,
    key_shard,
    value_shard,
    key_taps,
    value_taps,
    out_shard,
    frames_valid,
    out,
    tokens,
    normed,
    query_w,
    key_w,
    value_w,
    out_w,
    out_rows,
    key_partial,
    value_partial,
    query,
    key,
    value,
    memory_key,
    memory_value,
    spread_key,
    spread_value,
    shares,
    totals,
    heads,
    local_sems,
    send_sems,
    recv_sems,
):
    vid, tm = lax.axis_index("vid"), lax.axis_index("tm")
    core = lax.rem(vid, 2)
    place = {
        "x": tm // 8,
        "y": lax.rem(tm, 4),
        "z": lax.rem(tm // 4, 2) * 2 + vid // 2,
    }
    after, before = lax.rem(tm + 1, N_TM), lax.rem(tm + N_TM - 1, N_TM)
    partner = device(place, 1 - core)
    across = device(moved(place, "z", 2), core)

    barrier = pltpu.get_barrier_semaphore()
    greeted = [device(moved(place, axis, steps), core) for axis in "xyz" for steps in (1, -1)]
    greeted += [device(moved(place, axis, 2), core) for axis in "xyz"]
    greeted.append(partner)
    greeted.append(device(moved(moved(place, "x", -1), "y", -1), core))
    for other in greeted:
        pl.semaphore_signal(barrier, inc=1, device_id=other, device_id_type=MESH)

    shards = (query_shard, key_shard, value_shard, out_shard)
    weights = (query_w, key_w, value_w, out_w)
    own = [
        pltpu.make_async_copy(
            shard,
            weight.at[vid // 2, core, place["x"], place["z"] // 2, place["y"]],
            local_sems.at[k],
        )
        for k, (shard, weight) in enumerate(zip(shards, weights))
    ]
    own_tokens = pltpu.make_async_copy(video, tokens.at[pl.ds(SPATIAL, ROWS)], local_sems.at[4])
    for copy in own:
        copy.start()
    own_tokens.start()
    pl.semaphore_wait(barrier, len(greeted))

    wires = Wires(send_sems, recv_sems)
    key_value, query_part, out_part = (
        [Gather(wires, weights[p[0]], shards[p[0]], place, core, p) for p in stream]
        for stream in (KEY_VALUE, QUERY, OUT)
    )
    everything = key_value + query_part + out_part
    for gather in everything:
        gather.open()
    halo_slot = wires.slot()
    halo = tokens.at[pl.ds(0, SPATIAL)]

    last_frame = video.at[pl.ds(ROWS - SPATIAL, SPATIAL)]
    halo_copy = wires.send(halo_slot, last_frame, halo, (vid, after), start=False)

    @pl.when(place["y"] < 3)
    def _():
        halo_copy.start()

    for copy in own:
        copy.wait()
    own_tokens.wait()

    scale = gain[...].astype(jnp.float32).reshape(1, D)

    def normalize_at(i, carry):
        at = pl.ds(pl.multiple_of(i * 32, 32), 32)
        normed[at, :] = normalize_rows(tokens[at, :].astype(jnp.float32), scale)
        return carry

    lax.fori_loop(SPATIAL // 32, EXT // 32, normalize_at, 0)
    for gather in key_value:
        gather.spread()

    @pl.when(place["y"] == 3)
    def _():
        halo_copy.start()

    for gather in key_value:
        gather.rise()
        gather.hand(0)

    for number in range(4):
        for gather in key_value:
            gather.rows[number].relay()
    for gather in query_part:
        gather.spread()
    for gather in out_part:
        gather.spread(False)
    for gather in key_value:
        gather.hand(1)
        gather.hand(2)
    for gather in key_value:
        gather.close()
        gather.hand(3)
    for gather in query_part:
        gather.rise()
        gather.hand(0)
    wires.receive(halo_slot, halo, (vid, before))
    lax.fori_loop(0, SPATIAL // 32, normalize_at, 0)
    project(normed, 0, EXT, key_w, core, key_partial, None)
    project(normed, 0, EXT, value_w, core, value_partial, None)
    for gather in key_value:
        gather.take()
    for gather in query_part:
        gather.relay()
        gather.hand(1)
        gather.hand(2)
    project(normed, 0, EXT, key_w, 1 - core, key_partial, key)
    project(normed, 0, EXT, value_w, 1 - core, value_partial, value)

    limit = frames_valid[vid]
    first_frame = tm * FRAMES_DEV
    valid = [
        (first_frame + f - 1 < limit) & (first_frame + f - 1 >= 0) for f in range(FRAMES_DEV + 1)
    ]
    memories = []
    for source, taps, spread, ref in (
        (key, key_taps, spread_key, memory_key),
        (value, value_taps, spread_value, memory_value),
    ):
        pool(source, taps, valid, spread, ref, place)
        region = memory_view(ref, place, 0, WIDTH)
        slot = wires.slot()
        mine, other = (
            [
                Memory(wires, ref, place, core, order, number * HALF, own_plane)
                for number, order in enumerate(MEMORY_ORDERS)
            ]
            for own_plane in (True, False)
        )
        wires.send(slot, region, region, across)
        for part in mine:
            part.first.open()
        memories.append((ref, slot, mine, other))
        if ref is memory_key:
            for gather in query_part:
                gather.close()
                gather.hand(3)
    for gather in out_part:
        gather.rise(False)
        gather.last()
        gather.hand(0)

    (key_ref, key_slot, key_mine, key_other), (value_ref, value_slot, value_mine, value_other) = memories
    far_place = moved(place, "z", 2)
    for part in key_mine:
        part.first.close()
        part.second.open()
    wires.receive(key_slot, memory_view(key_ref, far_place, 0, WIDTH), across)
    for part in key_other:
        part.first.open()
    for part in value_mine:
        part.first.close()
    wires.receive(value_slot, memory_view(value_ref, far_place, 0, WIDTH), across)
    for part in value_other:
        part.first.open()
    for part in key_other:
        part.first.close()
        part.second.open()
    for part in value_mine:
        part.second.open()
    for part in key_mine:
        part.second.relay()
    for gather in query_part:
        gather.take()
    project(normed, SPATIAL, ROWS, query_w, core, key_partial, None)
    for part in value_other:
        part.first.close()
        part.second.open()
    for part in key_other:
        part.second.relay()
    project(normed, SPATIAL, ROWS, query_w, 1 - core, key_partial, query)
    for part in value_mine:
        part.second.relay()
    for gather in out_part:
        gather.relay()
        gather.hand(1)
        gather.hand(2)
    for part in key_mine + key_other:
        part.second.close()

    query_frame = lax.broadcasted_iota(jnp.int32, (ROWS, ROWS), 0) // SPATIAL
    key_frame = lax.broadcasted_iota(jnp.int32, (ROWS, ROWS), 1) // SPATIAL
    near = (key_frame <= query_frame) & (first_frame + key_frame < limit)
    near_bias = jnp.where(near, 0.0, NEG)
    index = lax.broadcasted_iota(jnp.int32, (1, N_TM * MEM_DEV), 1)
    far = (2 * (index // (SPATIAL // 4)) < limit) & (index // MEM_DEV <= tm)
    far_bias = jnp.where(far, 0.0, NEG)

    def weigh(h, carry):
        lanes = pl.ds(pl.multiple_of(h * HD, HD), HD)
        queries = query[:, lanes]
        far_keys = memory_key[:, :, :, :, lanes].reshape(N_TM * MEM_DEV, HD)
        near_scores = scores_of(queries, key[SPATIAL:, lanes]) * SCALE + near_bias
        far_scores = scores_of(queries, far_keys) * SCALE + far_bias
        top = jnp.maximum(
            jnp.max(near_scores, axis=-1, keepdims=True),
            jnp.max(far_scores, axis=-1, keepdims=True),
        )
        total = jnp.zeros((ROWS, 1), jnp.float32)
        for first, scores in ((0, near_scores), (ROWS, far_scores)):
            exps = jnp.exp2(scores - top)
            total = total + jnp.sum(exps, axis=-1, keepdims=True)
            shares[h, :, first : first + scores.shape[1]] = exps.astype(jnp.bfloat16)
        totals[h] = jnp.broadcast_to(total, (ROWS, HD))
        return carry

    lax.fori_loop(0, HEADS // 2, weigh, 0, unroll=2)
    for part in value_other:
        part.second.relay()
    lax.fori_loop(HEADS // 2, HEADS, weigh, 0, unroll=2)

    for gather in out_part:
        gather.close()
        gather.hand(3)
    for gather in out_part:
        gather.take()

    def out_tile(j, carry):
        columns = pl.ds(pl.multiple_of(j * 256, 256), 256)
        out_rows[:, columns] = (
            out_w[:, :, :, :, :, :, columns]
            .astype(jnp.float32)
            .reshape(WIDTH, 256)
            .astype(jnp.bfloat16)
        )
        return carry

    lax.fori_loop(0, D // 256, out_tile, 0)

    for part in value_mine + value_other:
        part.second.close()

    def mix(h, carry):
        lanes = pl.ds(pl.multiple_of(h * HD, HD), HD)
        near_values = value[SPATIAL:, lanes]
        far_values = memory_value[:, :, :, :, lanes].reshape(N_TM * MEM_DEV, HD)
        mixed = jnp.dot(shares[h, :, :ROWS], near_values, preferred_element_type=jnp.float32)
        mixed = mixed + jnp.dot(
            shares[h, :, ROWS:], far_values, preferred_element_type=jnp.float32
        )
        heads[:, lanes] = (mixed / totals[h]).astype(jnp.bfloat16)
        return carry

    lax.fori_loop(0, HEADS, mix, 0, unroll=4)
    row_frame = first_frame + lax.broadcasted_iota(jnp.int32, (ROWS, 1), 0) // SPATIAL

    def result_tile(j, carry):
        columns = pl.ds(pl.multiple_of(j * 512, 512), 512)
        result = jnp.dot(heads[...], out_rows[:, columns], preferred_element_type=jnp.float32)
        out[:, columns] = jnp.where(row_frame < limit, result, 0.0).astype(jnp.bfloat16)
        return carry

    lax.fori_loop(0, D // 512, result_tile, 0, unroll=2)
    wires.drain()


N_SLOTS = len(PIECES) * 26 + 1 + 2 * (1 + 4 * 7)


def on_device(
    video,
    norm_gain,
    query_weight,
    key_weight,
    value_weight,
    key_kernel,
    value_kernel,
    out_weight,
    frames_valid,
):
    bf16 = jnp.bfloat16
    gathered = (2, 2, 4, 2, 4)
    vmem = pl.BlockSpec(memory_space=pltpu.VMEM)
    hbm = pl.BlockSpec(memory_space=pl.ANY)
    result = pl.pallas_call(
        body,
        out_shape=jax.ShapeDtypeStruct((ROWS, D), bf16),
        in_specs=[
            hbm,
            vmem,
            hbm,
            hbm,
            hbm,
            vmem,
            vmem,
            hbm,
            pl.BlockSpec(memory_space=pltpu.SMEM),
        ],
        out_specs=vmem,
        scratch_shapes=[
            pltpu.VMEM((EXT, D), bf16),
            pltpu.VMEM((EXT, D), bf16),
            pltpu.VMEM((*gathered, 16, WIDTH), bf16),
            pltpu.VMEM((*gathered, 16, WIDTH), bf16),
            pltpu.VMEM((*gathered, 16, WIDTH), bf16),
            pltpu.VMEM((*gathered, 8, D), bf16),
            pltpu.VMEM((WIDTH, D), bf16),
            pltpu.VMEM((EXT, WIDTH), jnp.float32),
            pltpu.VMEM((EXT, WIDTH), jnp.float32),
            pltpu.VMEM((ROWS, WIDTH), bf16),
            pltpu.VMEM((EXT, WIDTH), bf16),
            pltpu.VMEM((EXT, WIDTH), bf16),
            pltpu.VMEM((4, 2, 4, MEM_DEV, WIDTH), bf16),
            pltpu.VMEM((4, 2, 4, MEM_DEV, WIDTH), bf16),
            pltpu.VMEM((HEADS, 2 * MEM_DEV, HD), jnp.float32),
            pltpu.VMEM((HEADS, 2 * MEM_DEV, HD), jnp.float32),
            pltpu.VMEM((HEADS, ROWS, KEYS), bf16),
            pltpu.VMEM((HEADS, ROWS, HD), jnp.float32),
            pltpu.VMEM((ROWS, WIDTH), bf16),
            pltpu.SemaphoreType.DMA((5,)),
            pltpu.SemaphoreType.DMA((N_SLOTS,)),
            pltpu.SemaphoreType.DMA((N_SLOTS,)),
        ],
        compiler_params=pltpu.CompilerParams(
            collective_id=0, has_side_effects=True, vmem_limit_bytes=60 * 1024 * 1024
        ),
        name="memory_attention",
    )(
        video[0],
        norm_gain,
        query_weight,
        key_weight,
        value_weight,
        key_kernel,
        value_kernel,
        out_weight,
        frames_valid,
    )
    return result[None]


def solution(mesh):
    in_specs = (
        P("vid", "tm", None),
        P(),
        P(("vid", "tm"), None),
        P(("vid", "tm"), None),
        P(("vid", "tm"), None),
        P(),
        P(),
        P(("vid", "tm"), None),
        P(),
    )
    out_specs = P("vid", "tm", None)
    return jax.shard_map(
        on_device, mesh=mesh, in_specs=in_specs, out_specs=out_specs, check_vma=False
    )
```

```python
import functools
import math

import jax
import jax.numpy as jnp
from jax import lax
from jax.experimental import pallas as pl
from jax.experimental.pallas import tpu as pltpu
from jax.sharding import PartitionSpec as P

MESH = pl.DeviceIdType.MESH
HEADS = 8
HD = 128
SIDE = 8
SPATIAL = SIDE * SIDE
N_TM = 32
ROWS = 256
FRAMES_DEV = ROWS // SPATIAL
EXT = ROWS + SPATIAL
MEM_DEV = 32
D = 2048
WIDTH = HEADS * HD
NEG = -1e30
SCALE = (1.0 / math.sqrt(HD)) * math.log2(math.e)

KEY_VALUE = (
    (1, 0, 768, "xyz"),
    (1, 768, 256, "yzx"),
    (2, 0, 384, "yzx"),
    (2, 384, 640, "zxy"),
)
QUERY = ((0, 0, 384, "xyz"), (0, 384, 384, "yzx"), (0, 768, 256, "zxy"))
OUT = ((3, 0, 1024, "xyz"), (3, 1024, 1024, "yxz"))
PIECES = KEY_VALUE + QUERY + OUT
HALF = WIDTH // 2
MEMORY_ORDERS = ("xy", "yx")
KEYS = ROWS + N_TM * MEM_DEV


def device(place, core):
    x, y, z = place["x"], place["y"], place["z"]
    return (lax.rem(z, 2) * 2 + core, x * 8 + (z // 2) * 4 + y)


def moved(place, axis, steps):
    return {**place, axis: lax.rem(place[axis] + steps + 4, 4)}


def halves(start, size):
    first = (size // 256) * 128 if size > 128 else size
    return ((start, first), (start + first, size - first))


class Wires:
    def __init__(self, send_sems, recv_sems):
        self.send_sems, self.recv_sems = send_sems, recv_sems
        self.count = 0
        self.started = []

    def slot(self):
        self.count += 1
        return self.count - 1

    def send(self, slot, src, dst, target, start=True):
        copy = pltpu.make_async_remote_copy(
            src_ref=src,
            dst_ref=dst,
            send_sem=self.send_sems.at[slot],
            recv_sem=self.recv_sems.at[slot],
            device_id=target,
            device_id_type=MESH,
        )
        if start:
            copy.start()
        self.started.append(copy)
        return copy

    def receive(self, slot, dst, source):
        pltpu.make_async_remote_copy(
            src_ref=dst,
            dst_ref=dst,
            send_sem=self.send_sems.at[slot],
            recv_sem=self.recv_sems.at[slot],
            device_id=source,
            device_id_type=MESH,
        ).wait_recv()

    def drain(self):
        for copy in self.started:
            copy.wait_send()


def weight_view(ref, core, place, start, size):
    every = slice(None)
    x, y, z = (place[axis] for axis in "xyz")
    zl = every if z is None else lax.rem(z, 2)
    zh = every if z is None else z // 2
    return ref.at[
        zl,
        core,
        every if x is None else x,
        zh,
        every if y is None else y,
        :,
        pl.ds(start, size),
    ]


def memory_view(ref, place, start, size):
    every = slice(None)
    x, y, z = (place[axis] for axis in "xyz")
    return ref.at[
        every if x is None else x,
        every if z is None else z // 2,
        every if y is None else y,
        :,
        pl.ds(start, size),
    ]


class Phase:
    def __init__(self, wires, view, place, core, axis, known, start, size, source=None):
        self.wires, self.view, self.place, self.core = wires, view, place, core
        self.axis, self.known, self.start, self.size = axis, known, start, size
        self.source = place if source is None else source
        self.slots = [wires.slot() for _ in range(self.count)]

    def region(self, steps, start, size):
        place = {**moved(self.source, self.axis, steps), **{a: None for a in self.known}}
        return self.view(place, start, size)

    def target(self, steps):
        return device(moved(self.place, self.axis, steps), self.core)

    def send(self, number, steps, part, src=None, of=0):
        region = self.region(of, *part)
        src = region if src is None else src
        self.wires.send(self.slots[number], src, region, self.target(steps))

    def receive(self, number, steps, part, of):
        self.wires.receive(self.slots[number], self.region(of, *part), self.target(-steps))


class Direct(Phase):
    count = 3

    def open(self, src=None):
        for number, steps in enumerate((1, -1, 2)):
            self.send(number, steps, (self.start, self.size), src)

    def take(self, number):
        steps = (1, -1, 2)[number]
        self.receive(number, steps, (self.start, self.size), -steps)

    def close(self):
        for number in range(3):
            self.take(number)


class Ring(Phase):
    count = 4

    def open(self):
        for number, steps in enumerate((1, -1)):
            self.send(number, steps, (self.start, self.size))

    def relay(self):
        parts = halves(self.start, self.size)
        for number, steps in enumerate((1, -1)):
            self.receive(number, steps, (self.start, self.size), -steps)
            self.send(number + 2, steps, parts[number], of=-steps)

    def close(self):
        parts = halves(self.start, self.size)
        for number, steps in enumerate((1, -1)):
            self.receive(number + 2, steps, parts[number], 2)


class Gather:
    def __init__(self, wires, ref, shard, place, core, piece):
        _, self.start, self.size, order = piece
        self.wires, self.ref, self.shard = wires, ref, shard
        self.place, self.core, self.order = place, core, order
        self.partner = device(place, 1 - core)
        common = (
            wires,
            lambda at, start, size: weight_view(ref, core, at, start, size),
            place,
            core,
        )
        first, second, third = order
        self.first = Direct(*common, first, "", self.start, self.size)
        self.second = Direct(*common, second, first, self.start, self.size)
        self.rows = [
            Ring(*common, third, first, self.start, self.size, moved(place, second, steps))
            for steps in (0, -1, 1, 2)
        ]
        self.slots = [wires.slot() for _ in range(4)]

    def open(self):
        self.first.open(self.shard.at[:, pl.ds(self.start, self.size)])

    def spread(self, on=True):
        self.first.close()
        self.second.open()
        if on:
            self.rows[0].open()

    def rise(self, on=True):
        for number in range(3):
            self.second.take(number)
            if on:
                self.rows[number + 1].open()

    def last(self):
        for row in self.rows:
            row.open()

    def relay(self):
        for row in self.rows:
            row.relay()

    def close(self):
        for row in self.rows:
            row.close()

    def region(self, core, steps):
        place = {
            **moved(self.place, self.order[2], steps),
            self.order[0]: None,
            self.order[1]: None,
        }
        return weight_view(self.ref, core, place, self.start, self.size)

    def hand(self, k):
        region = self.region(self.core, (0, 1, -1, 2)[k])
        self.wires.send(self.slots[k], region, region, self.partner)

    def take(self):
        for k, steps in enumerate((0, 1, -1, 2)):
            self.wires.receive(self.slots[k], self.region(1 - self.core, steps), self.partner)


def normalize_rows(values, gain):
    center = jnp.mean(values, axis=-1, keepdims=True)
    spread = jnp.mean((values - center) ** 2, axis=-1, keepdims=True)
    return ((values - center) * lax.rsqrt(spread + 1e-06) * gain).astype(jnp.bfloat16)


def project(normed, first, count, weight, core, partial, out):
    def tile(j, carry):
        columns = pl.ds(pl.multiple_of(j * 256, 256), 256)
        total = jnp.zeros((count, 256), jnp.float32) if out is None else partial[:count, columns]
        for zl in range(2):
            rows = weight[zl, core, :, :, :, :, columns].reshape(512, 256)
            depth = pl.ds(pl.multiple_of((zl * 2 + core) * 512, 512), 512)
            total = total + jnp.dot(
                normed[first : first + count, depth], rows, preferred_element_type=jnp.float32
            )
        if out is None:
            partial[:count, columns] = total
        else:
            out[:, columns] = total.astype(jnp.bfloat16)
        return carry

    lax.fori_loop(0, WIDTH // 256, tile, 0, unroll=2)


def pool(source, taps, valid, spread_tmp, out, place):
    column = lax.broadcasted_iota(jnp.int32, (SIDE, HD), 0)

    def head(h, carry):
        lanes = pl.ds(pl.multiple_of(h * HD, HD), HD)
        grid = source[:, lanes].astype(jnp.float32).reshape(FRAMES_DEV + 1, SIDE, SIDE, HD)
        kernel = taps[:, lanes].astype(jnp.float32)
        frames = [jnp.where(valid[f], grid[f], 0.0) for f in range(FRAMES_DEV + 1)]
        for j in range(FRAMES_DEV // 2):
            for a in range(SIDE // 2):
                sums = [jnp.zeros((SIDE, HD), jnp.float32) for _ in range(3)]
                for dt in range(3):
                    for dh in range(3):
                        row = 2 * a + dh - 1
                        if row < 0:
                            continue
                        values = frames[2 * j + 2 - dt][row]
                        for dw in range(3):
                            tap = 9 * dt + 3 * dh + dw
                            sums[dw] = sums[dw] + values * kernel[tap : tap + 1]
                left = jnp.where(column == 0, 0.0, pltpu.roll(sums[0], 1, 0))
                right = pltpu.roll(sums[2], SIDE - 1, 0)
                at = (j * (SIDE // 2) + a) * SIDE
                spread_tmp[h, at : at + SIDE, :] = sums[1] + left + right
        rows = spread_tmp[h, pl.ds(0, MEM_DEV, stride=2), :]
        center = jnp.mean(rows, axis=-1, keepdims=True)
        width = jnp.mean((rows - center) ** 2, axis=-1, keepdims=True)
        normed = (rows - center) * lax.rsqrt(width + 1e-06)
        out[place["x"], place["z"] // 2, place["y"], :, lanes] = normed.astype(jnp.bfloat16)
        return carry

    lax.fori_loop(0, HEADS, head, 0, unroll=2)


def scores_of(queries, keys):
    return lax.dot_general(
        queries, keys, (((1,), (1,)), ((), ())), preferred_element_type=jnp.float32
    )


class Memory:
    def __init__(self, wires, ref, place, core, order, start, own):
        common = (
            wires,
            lambda at, first, size: memory_view(ref, at, first, size),
            place,
            core,
        )
        source = place if own else moved(place, "z", 2)
        self.first = Direct(*common, order[0], "", start, HALF, source)
        self.second = Ring(*common, order[1], order[0], start, HALF, source)


def body(
    video,
    gain,
    query_shard,
    key_shard,
    value_shard,
    key_taps,
    value_taps,
    out_shard,
    frames_valid,
    out,
    tokens,
    normed,
    query_w,
    key_w,
    value_w,
    out_w,
    out_rows,
    key_partial,
    value_partial,
    query,
    key,
    value,
    memory_key,
    memory_value,
    spread_key,
    spread_value,
    shares,
    totals,
    heads,
    local_sems,
    send_sems,
    recv_sems,
):
    vid, tm = lax.axis_index("vid"), lax.axis_index("tm")
    core = lax.rem(vid, 2)
    place = {
        "x": tm // 8,
        "y": lax.rem(tm, 4),
        "z": lax.rem(tm // 4, 2) * 2 + vid // 2,
    }
    after, before = lax.rem(tm + 1, N_TM), lax.rem(tm + N_TM - 1, N_TM)
    partner = device(place, 1 - core)
    across = device(moved(place, "z", 2), core)

    barrier = pltpu.get_barrier_semaphore()
    greeted = [device(moved(place, axis, steps), core) for axis in "xyz" for steps in (1, -1)]
    greeted += [device(moved(place, axis, 2), core) for axis in "xyz"]
    greeted.append(partner)
    greeted.append(device(moved(moved(place, "x", -1), "y", -1), core))
    for other in greeted:
        pl.semaphore_signal(barrier, inc=1, device_id=other, device_id_type=MESH)

    shards = (query_shard, key_shard, value_shard, out_shard)
    weights = (query_w, key_w, value_w, out_w)
    own = [
        pltpu.make_async_copy(
            shard,
            weight.at[vid // 2, core, place["x"], place["z"] // 2, place["y"]],
            local_sems.at[k],
        )
        for k, (shard, weight) in enumerate(zip(shards, weights))
    ]
    own_tokens = pltpu.make_async_copy(video, tokens.at[pl.ds(SPATIAL, ROWS)], local_sems.at[4])
    for copy in own:
        copy.start()
    own_tokens.start()
    pl.semaphore_wait(barrier, len(greeted))

    wires = Wires(send_sems, recv_sems)
    key_value, query_part, out_part = (
        [Gather(wires, weights[p[0]], shards[p[0]], place, core, p) for p in stream]
        for stream in (KEY_VALUE, QUERY, OUT)
    )
    everything = key_value + query_part + out_part
    for gather in everything:
        gather.open()
    halo_slot = wires.slot()
    halo = tokens.at[pl.ds(0, SPATIAL)]

    last_frame = video.at[pl.ds(ROWS - SPATIAL, SPATIAL)]
    halo_copy = wires.send(halo_slot, last_frame, halo, (vid, after), start=False)

    @pl.when(place["y"] < 3)
    def _():
        halo_copy.start()

    for copy in own:
        copy.wait()
    own_tokens.wait()

    scale = gain[...].astype(jnp.float32).reshape(1, D)

    def normalize_at(i, carry):
        at = pl.ds(pl.multiple_of(i * 32, 32), 32)
        normed[at, :] = normalize_rows(tokens[at, :].astype(jnp.float32), scale)
        return carry

    lax.fori_loop(SPATIAL // 32, EXT // 32, normalize_at, 0)
    for gather in key_value:
        gather.spread()

    @pl.when(place["y"] == 3)
    def _():
        halo_copy.start()

    for gather in key_value:
        gather.rise()
        gather.hand(0)

    for number in range(4):
        for gather in key_value:
            gather.rows[number].relay()
    for gather in query_part:
        gather.spread()
    for gather in out_part:
        gather.spread(False)
    for gather in key_value:
        gather.hand(1)
        gather.hand(2)
    for gather in key_value:
        gather.close()
        gather.hand(3)
    for gather in query_part:
        gather.rise()
        gather.hand(0)
    wires.receive(halo_slot, halo, (vid, before))
    lax.fori_loop(0, SPATIAL // 32, normalize_at, 0)
    project(normed, 0, EXT, key_w, core, key_partial, None)
    project(normed, 0, EXT, value_w, core, value_partial, None)
    for gather in key_value:
        gather.take()
    for gather in query_part:
        gather.relay()
        gather.hand(1)
        gather.hand(2)
    project(normed, 0, EXT, key_w, 1 - core, key_partial, key)
    project(normed, 0, EXT, value_w, 1 - core, value_partial, value)

    limit = frames_valid[vid]
    first_frame = tm * FRAMES_DEV
    valid = [
        (first_frame + f - 1 < limit) & (first_frame + f - 1 >= 0) for f in range(FRAMES_DEV + 1)
    ]
    memories = []
    for source, taps, spread, ref in (
        (key, key_taps, spread_key, memory_key),
        (value, value_taps, spread_value, memory_value),
    ):
        pool(source, taps, valid, spread, ref, place)
        region = memory_view(ref, place, 0, WIDTH)
        slot = wires.slot()
        mine, other = (
            [
                Memory(wires, ref, place, core, order, number * HALF, own_plane)
                for number, order in enumerate(MEMORY_ORDERS)
            ]
            for own_plane in (True, False)
        )
        wires.send(slot, region, region, across)
        for part in mine:
            part.first.open()
        memories.append((ref, slot, mine, other))
        if ref is memory_key:
            for gather in query_part:
                gather.close()
                gather.hand(3)
    for gather in out_part:
        gather.rise(False)
        gather.last()
        gather.hand(0)

    (key_ref, key_slot, key_mine, key_other), (value_ref, value_slot, value_mine, value_other) = memories
    far_place = moved(place, "z", 2)
    for part in key_mine:
        part.first.close()
        part.second.open()
    wires.receive(key_slot, memory_view(key_ref, far_place, 0, WIDTH), across)
    for part in key_other:
        part.first.open()
    for part in value_mine:
        part.first.close()
    wires.receive(value_slot, memory_view(value_ref, far_place, 0, WIDTH), across)
    for part in value_other:
        part.first.open()
    for part in key_other:
        part.first.close()
        part.second.open()
    for part in value_mine:
        part.second.open()
    for part in key_mine:
        part.second.relay()
    for gather in query_part:
        gather.take()
    project(normed, SPATIAL, ROWS, query_w, core, key_partial, None)
    for part in value_other:
        part.first.close()
        part.second.open()
    for part in key_other:
        part.second.relay()
    project(normed, SPATIAL, ROWS, query_w, 1 - core, key_partial, query)
    for part in value_mine:
        part.second.relay()
    for gather in out_part:
        gather.relay()
        gather.hand(1)
        gather.hand(2)
    for part in key_mine + key_other:
        part.second.close()

    query_frame = lax.broadcasted_iota(jnp.int32, (ROWS, ROWS), 0) // SPATIAL
    key_frame = lax.broadcasted_iota(jnp.int32, (ROWS, ROWS), 1) // SPATIAL
    near = (key_frame <= query_frame) & (first_frame + key_frame < limit)
    near_bias = jnp.where(near, 0.0, NEG)
    index = lax.broadcasted_iota(jnp.int32, (1, N_TM * MEM_DEV), 1)
    far = (2 * (index // (SPATIAL // 4)) < limit) & (index // MEM_DEV <= tm)
    far_bias = jnp.where(far, 0.0, NEG)

    def weigh(h, carry):
        lanes = pl.ds(pl.multiple_of(h * HD, HD), HD)
        queries = query[:, lanes]
        far_keys = memory_key[:, :, :, :, lanes].reshape(N_TM * MEM_DEV, HD)
        near_scores = scores_of(queries, key[SPATIAL:, lanes]) * SCALE + near_bias
        far_scores = scores_of(queries, far_keys) * SCALE + far_bias
        top = jnp.maximum(
            jnp.max(near_scores, axis=-1, keepdims=True),
            jnp.max(far_scores, axis=-1, keepdims=True),
        )
        total = jnp.zeros((ROWS, 1), jnp.float32)
        for first, scores in ((0, near_scores), (ROWS, far_scores)):
            exps = jnp.exp2(scores - top)
            total = total + jnp.sum(exps, axis=-1, keepdims=True)
            shares[h, :, first : first + scores.shape[1]] = exps.astype(jnp.bfloat16)
        totals[h] = jnp.broadcast_to(total, (ROWS, HD))
        return carry

    lax.fori_loop(0, HEADS // 2, weigh, 0, unroll=2)
    for part in value_other:
        part.second.relay()
    lax.fori_loop(HEADS // 2, HEADS, weigh, 0, unroll=2)

    for gather in out_part:
        gather.close()
        gather.hand(3)
    for gather in out_part:
        gather.take()

    def out_tile(j, carry):
        columns = pl.ds(pl.multiple_of(j * 256, 256), 256)
        out_rows[:, columns] = (
            out_w[:, :, :, :, :, :, columns]
            .astype(jnp.float32)
            .reshape(WIDTH, 256)
            .astype(jnp.bfloat16)
        )
        return carry

    lax.fori_loop(0, D // 256, out_tile, 0)

    for part in value_mine + value_other:
        part.second.close()

    def mix(h, carry):
        lanes = pl.ds(pl.multiple_of(h * HD, HD), HD)
        near_values = value[SPATIAL:, lanes]
        far_values = memory_value[:, :, :, :, lanes].reshape(N_TM * MEM_DEV, HD)
        mixed = jnp.dot(shares[h, :, :ROWS], near_values, preferred_element_type=jnp.float32)
        mixed = mixed + jnp.dot(
            shares[h, :, ROWS:], far_values, preferred_element_type=jnp.float32
        )
        heads[:, lanes] = (mixed / totals[h]).astype(jnp.bfloat16)
        return carry

    lax.fori_loop(0, HEADS, mix, 0, unroll=4)
    row_frame = first_frame + lax.broadcasted_iota(jnp.int32, (ROWS, 1), 0) // SPATIAL

    def result_tile(j, carry):
        columns = pl.ds(pl.multiple_of(j * 512, 512), 512)
        result = jnp.dot(heads[...], out_rows[:, columns], preferred_element_type=jnp.float32)
        out[:, columns] = jnp.where(row_frame < limit, result, 0.0).astype(jnp.bfloat16)
        return carry

    lax.fori_loop(0, D // 512, result_tile, 0, unroll=2)
    wires.drain()


N_SLOTS = len(PIECES) * 26 + 1 + 2 * (1 + 4 * 7)


def on_device(
    video,
    norm_gain,
    query_weight,
    key_weight,
    value_weight,
    key_kernel,
    value_kernel,
    out_weight,
    frames_valid,
):
    bf16 = jnp.bfloat16
    gathered = (2, 2, 4, 2, 4)
    vmem = pl.BlockSpec(memory_space=pltpu.VMEM)
    hbm = pl.BlockSpec(memory_space=pl.ANY)
    result = pl.pallas_call(
        body,
        out_shape=jax.ShapeDtypeStruct((ROWS, D), bf16),
        in_specs=[
            hbm,
            vmem,
            hbm,
            hbm,
            hbm,
            vmem,
            vmem,
            hbm,
            pl.BlockSpec(memory_space=pltpu.SMEM),
        ],
        out_specs=vmem,
        scratch_shapes=[
            pltpu.VMEM((EXT, D), bf16),
            pltpu.VMEM((EXT, D), bf16),
            pltpu.VMEM((*gathered, 16, WIDTH), bf16),
            pltpu.VMEM((*gathered, 16, WIDTH), bf16),
            pltpu.VMEM((*gathered, 16, WIDTH), bf16),
            pltpu.VMEM((*gathered, 8, D), bf16),
            pltpu.VMEM((WIDTH, D), bf16),
            pltpu.VMEM((EXT, WIDTH), jnp.float32),
            pltpu.VMEM((EXT, WIDTH), jnp.float32),
            pltpu.VMEM((ROWS, WIDTH), bf16),
            pltpu.VMEM((EXT, WIDTH), bf16),
            pltpu.VMEM((EXT, WIDTH), bf16),
            pltpu.VMEM((4, 2, 4, MEM_DEV, WIDTH), bf16),
            pltpu.VMEM((4, 2, 4, MEM_DEV, WIDTH), bf16),
            pltpu.VMEM((HEADS, 2 * MEM_DEV, HD), jnp.float32),
            pltpu.VMEM((HEADS, 2 * MEM_DEV, HD), jnp.float32),
            pltpu.VMEM((HEADS, ROWS, KEYS), bf16),
            pltpu.VMEM((HEADS, ROWS, HD), jnp.float32),
            pltpu.VMEM((ROWS, WIDTH), bf16),
            pltpu.SemaphoreType.DMA((5,)),
            pltpu.SemaphoreType.DMA((N_SLOTS,)),
            pltpu.SemaphoreType.DMA((N_SLOTS,)),
        ],
        compiler_params=pltpu.CompilerParams(
            collective_id=0, has_side_effects=True, vmem_limit_bytes=60 * 1024 * 1024
        ),
        name="memory_attention",
    )(
        video[0],
        norm_gain,
        query_weight,
        key_weight,
        value_weight,
        key_kernel,
        value_kernel,
        out_weight,
        frames_valid,
    )
    return result[None]


def solution(mesh):
    in_specs = (
        P("vid", "tm", None),
        P(),
        P(("vid", "tm"), None),
        P(("vid", "tm"), None),
        P(("vid", "tm"), None),
        P(),
        P(),
        P(("vid", "tm"), None),
        P(),
    )
    out_specs = P("vid", "tm", None)
    return jax.shard_map(
        on_device, mesh=mesh, in_specs=in_specs, out_specs=out_specs, check_vma=False
    )
```

```python
import functools
import math

import jax
import jax.numpy as jnp
from jax import lax
from jax.experimental import pallas as pl
from jax.experimental.pallas import tpu as pltpu
from jax.sharding import PartitionSpec as P

MESH = pl.DeviceIdType.MESH
HEADS = 8
HD = 128
SIDE = 8
SPATIAL = SIDE * SIDE
N_TM = 32
ROWS = 256
FRAMES_DEV = ROWS // SPATIAL
EXT = ROWS + SPATIAL
MEM_DEV = 32
D = 2048
WIDTH = HEADS * HD
NEG = -1e30
SCALE = (1.0 / math.sqrt(HD)) * math.log2(math.e)

KEY_VALUE = (
    (1, 0, 768, "xyz"),
    (1, 768, 256, "yzx"),
    (2, 0, 384, "yzx"),
    (2, 384, 640, "zxy"),
)
QUERY = ((0, 0, 384, "xyz"), (0, 384, 384, "yzx"), (0, 768, 256, "zxy"))
OUT = ((3, 0, 1024, "xyz"), (3, 1024, 1024, "yxz"))
PIECES = KEY_VALUE + QUERY + OUT
HALF = WIDTH // 2
MEMORY_ORDERS = ("xy", "yx")
KEYS = ROWS + N_TM * MEM_DEV


def device(place, core):
    x, y, z = place["x"], place["y"], place["z"]
    return (lax.rem(z, 2) * 2 + core, x * 8 + (z // 2) * 4 + y)


def moved(place, axis, steps):
    return {**place, axis: lax.rem(place[axis] + steps + 4, 4)}


def halves(start, size):
    first = (size // 256) * 128 if size > 128 else size
    return ((start, first), (start + first, size - first))


class Wires:
    def __init__(self, send_sems, recv_sems):
        self.send_sems, self.recv_sems = send_sems, recv_sems
        self.count = 0
        self.started = []

    def slot(self):
        self.count += 1
        return self.count - 1

    def send(self, slot, src, dst, target, start=True):
        copy = pltpu.make_async_remote_copy(
            src_ref=src,
            dst_ref=dst,
            send_sem=self.send_sems.at[slot],
            recv_sem=self.recv_sems.at[slot],
            device_id=target,
            device_id_type=MESH,
        )
        if start:
            copy.start()
        self.started.append(copy)
        return copy

    def receive(self, slot, dst, source):
        pltpu.make_async_remote_copy(
            src_ref=dst,
            dst_ref=dst,
            send_sem=self.send_sems.at[slot],
            recv_sem=self.recv_sems.at[slot],
            device_id=source,
            device_id_type=MESH,
        ).wait_recv()

    def drain(self):
        for copy in self.started:
            copy.wait_send()


def weight_view(ref, core, place, start, size):
    every = slice(None)
    x, y, z = (place[axis] for axis in "xyz")
    zl = every if z is None else lax.rem(z, 2)
    zh = every if z is None else z // 2
    return ref.at[
        zl,
        core,
        every if x is None else x,
        zh,
        every if y is None else y,
        :,
        pl.ds(start, size),
    ]


def memory_view(ref, place, start, size):
    every = slice(None)
    x, y, z = (place[axis] for axis in "xyz")
    return ref.at[
        every if x is None else x,
        every if z is None else z // 2,
        every if y is None else y,
        :,
        pl.ds(start, size),
    ]


class Phase:
    def __init__(self, wires, view, place, core, axis, known, start, size, source=None):
        self.wires, self.view, self.place, self.core = wires, view, place, core
        self.axis, self.known, self.start, self.size = axis, known, start, size
        self.source = place if source is None else source
        self.slots = [wires.slot() for _ in range(self.count)]

    def region(self, steps, start, size):
        place = {**moved(self.source, self.axis, steps), **{a: None for a in self.known}}
        return self.view(place, start, size)

    def target(self, steps):
        return device(moved(self.place, self.axis, steps), self.core)

    def send(self, number, steps, part, src=None, of=0):
        region = self.region(of, *part)
        src = region if src is None else src
        self.wires.send(self.slots[number], src, region, self.target(steps))

    def receive(self, number, steps, part, of):
        self.wires.receive(self.slots[number], self.region(of, *part), self.target(-steps))


class Direct(Phase):
    count = 3

    def open(self, src=None):
        for number, steps in enumerate((1, -1, 2)):
            self.send(number, steps, (self.start, self.size), src)

    def take(self, number):
        steps = (1, -1, 2)[number]
        self.receive(number, steps, (self.start, self.size), -steps)

    def close(self):
        for number in range(3):
            self.take(number)


class Ring(Phase):
    count = 4

    def open(self):
        for number, steps in enumerate((1, -1)):
            self.send(number, steps, (self.start, self.size))

    def relay(self):
        parts = halves(self.start, self.size)
        for number, steps in enumerate((1, -1)):
            self.receive(number, steps, (self.start, self.size), -steps)
            self.send(number + 2, steps, parts[number], of=-steps)

    def close(self):
        parts = halves(self.start, self.size)
        for number, steps in enumerate((1, -1)):
            self.receive(number + 2, steps, parts[number], 2)


class Gather:
    def __init__(self, wires, ref, shard, place, core, piece):
        _, self.start, self.size, order = piece
        self.wires, self.ref, self.shard = wires, ref, shard
        self.place, self.core, self.order = place, core, order
        self.partner = device(place, 1 - core)
        common = (
            wires,
            lambda at, start, size: weight_view(ref, core, at, start, size),
            place,
            core,
        )
        first, second, third = order
        self.first = Direct(*common, first, "", self.start, self.size)
        self.second = Direct(*common, second, first, self.start, self.size)
        self.rows = [
            Ring(*common, third, first, self.start, self.size, moved(place, second, steps))
            for steps in (0, -1, 1, 2)
        ]
        self.slots = [wires.slot() for _ in range(4)]

    def open(self):
        self.first.open(self.shard.at[:, pl.ds(self.start, self.size)])

    def spread(self, on=True):
        self.first.close()
        self.second.open()
        if on:
            self.rows[0].open()

    def rise(self, on=True):
        for number in range(3):
            self.second.take(number)
            if on:
                self.rows[number + 1].open()

    def last(self):
        for row in self.rows:
            row.open()

    def relay(self):
        for row in self.rows:
            row.relay()

    def close(self):
        for row in self.rows:
            row.close()

    def region(self, core, steps):
        place = {
            **moved(self.place, self.order[2], steps),
            self.order[0]: None,
            self.order[1]: None,
        }
        return weight_view(self.ref, core, place, self.start, self.size)

    def hand(self, k):
        region = self.region(self.core, (0, 1, -1, 2)[k])
        self.wires.send(self.slots[k], region, region, self.partner)

    def take(self):
        for k, steps in enumerate((0, 1, -1, 2)):
            self.wires.receive(self.slots[k], self.region(1 - self.core, steps), self.partner)


def normalize_rows(values, gain):
    center = jnp.mean(values, axis=-1, keepdims=True)
    spread = jnp.mean((values - center) ** 2, axis=-1, keepdims=True)
    return ((values - center) * lax.rsqrt(spread + 1e-06) * gain).astype(jnp.bfloat16)


def project(normed, first, count, weight, core, partial, out):
    def tile(j, carry):
        columns = pl.ds(pl.multiple_of(j * 256, 256), 256)
        total = jnp.zeros((count, 256), jnp.float32) if out is None else partial[:count, columns]
        for zl in range(2):
            rows = weight[zl, core, :, :, :, :, columns].reshape(512, 256)
            depth = pl.ds(pl.multiple_of((zl * 2 + core) * 512, 512), 512)
            total = total + jnp.dot(
                normed[first : first + count, depth], rows, preferred_element_type=jnp.float32
            )
        if out is None:
            partial[:count, columns] = total
        else:
            out[:, columns] = total.astype(jnp.bfloat16)
        return carry

    lax.fori_loop(0, WIDTH // 256, tile, 0, unroll=4)


def pool(source, taps, valid, spread_tmp, out, place):
    column = lax.broadcasted_iota(jnp.int32, (SIDE, HD), 0)

    def head(h, carry):
        lanes = pl.ds(pl.multiple_of(h * HD, HD), HD)
        grid = source[:, lanes].astype(jnp.float32).reshape(FRAMES_DEV + 1, SIDE, SIDE, HD)
        kernel = taps[:, lanes].astype(jnp.float32)
        frames = [jnp.where(valid[f], grid[f], 0.0) for f in range(FRAMES_DEV + 1)]
        for j in range(FRAMES_DEV // 2):
            for a in range(SIDE // 2):
                sums = [jnp.zeros((SIDE, HD), jnp.float32) for _ in range(3)]
                for dt in range(3):
                    for dh in range(3):
                        row = 2 * a + dh - 1
                        if row < 0:
                            continue
                        values = frames[2 * j + 2 - dt][row]
                        for dw in range(3):
                            tap = 9 * dt + 3 * dh + dw
                            sums[dw] = sums[dw] + values * kernel[tap : tap + 1]
                left = jnp.where(column == 0, 0.0, pltpu.roll(sums[0], 1, 0))
                right = pltpu.roll(sums[2], SIDE - 1, 0)
                at = (j * (SIDE // 2) + a) * SIDE
                spread_tmp[h, at : at + SIDE, :] = sums[1] + left + right
        rows = spread_tmp[h, pl.ds(0, MEM_DEV, stride=2), :]
        center = jnp.mean(rows, axis=-1, keepdims=True)
        width = jnp.mean((rows - center) ** 2, axis=-1, keepdims=True)
        normed = (rows - center) * lax.rsqrt(width + 1e-06)
        out[place["x"], place["z"] // 2, place["y"], :, lanes] = normed.astype(jnp.bfloat16)
        return carry

    lax.fori_loop(0, HEADS, head, 0, unroll=4)


def scores_of(queries, keys):
    return lax.dot_general(
        queries, keys, (((1,), (1,)), ((), ())), preferred_element_type=jnp.float32
    )


class Memory:
    def __init__(self, wires, ref, place, core, order, start, own):
        common = (
            wires,
            lambda at, first, size: memory_view(ref, at, first, size),
            place,
            core,
        )
        source = place if own else moved(place, "z", 2)
        self.first = Direct(*common, order[0], "", start, HALF, source)
        self.second = Ring(*common, order[1], order[0], start, HALF, source)


def body(
    video,
    gain,
    query_shard,
    key_shard,
    value_shard,
    key_taps,
    value_taps,
    out_shard,
    frames_valid,
    out,
    tokens,
    normed,
    query_w,
    key_w,
    value_w,
    out_w,
    out_rows,
    key_partial,
    value_partial,
    query,
    key,
    value,
    memory_key,
    memory_value,
    spread_key,
    spread_value,
    shares,
    totals,
    heads,
    local_sems,
    send_sems,
    recv_sems,
):
    vid, tm = lax.axis_index("vid"), lax.axis_index("tm")
    core = lax.rem(vid, 2)
    place = {
        "x": tm // 8,
        "y": lax.rem(tm, 4),
        "z": lax.rem(tm // 4, 2) * 2 + vid // 2,
    }
    after, before = lax.rem(tm + 1, N_TM), lax.rem(tm + N_TM - 1, N_TM)
    partner = device(place, 1 - core)
    across = device(moved(place, "z", 2), core)

    barrier = pltpu.get_barrier_semaphore()
    greeted = [device(moved(place, axis, steps), core) for axis in "xyz" for steps in (1, -1)]
    greeted += [device(moved(place, axis, 2), core) for axis in "xyz"]
    greeted.append(partner)
    greeted.append(device(moved(moved(place, "x", -1), "y", -1), core))
    for other in greeted:
        pl.semaphore_signal(barrier, inc=1, device_id=other, device_id_type=MESH)

    shards = (query_shard, key_shard, value_shard, out_shard)
    weights = (query_w, key_w, value_w, out_w)
    own = [
        pltpu.make_async_copy(
            shard,
            weight.at[vid // 2, core, place["x"], place["z"] // 2, place["y"]],
            local_sems.at[k],
        )
        for k, (shard, weight) in enumerate(zip(shards, weights))
    ]
    own_tokens = pltpu.make_async_copy(video, tokens.at[pl.ds(SPATIAL, ROWS)], local_sems.at[4])
    for copy in own:
        copy.start()
    own_tokens.start()
    pl.semaphore_wait(barrier, len(greeted))

    wires = Wires(send_sems, recv_sems)
    key_value, query_part, out_part = (
        [Gather(wires, weights[p[0]], shards[p[0]], place, core, p) for p in stream]
        for stream in (KEY_VALUE, QUERY, OUT)
    )
    everything = key_value + query_part + out_part
    for gather in everything:
        gather.open()
    halo_slot = wires.slot()
    halo = tokens.at[pl.ds(0, SPATIAL)]

    last_frame = video.at[pl.ds(ROWS - SPATIAL, SPATIAL)]
    halo_copy = wires.send(halo_slot, last_frame, halo, (vid, after), start=False)

    @pl.when(place["y"] < 3)
    def _():
        halo_copy.start()

    for copy in own:
        copy.wait()
    own_tokens.wait()

    scale = gain[...].astype(jnp.float32).reshape(1, D)

    def normalize_at(i, carry):
        at = pl.ds(pl.multiple_of(i * 32, 32), 32)
        normed[at, :] = normalize_rows(tokens[at, :].astype(jnp.float32), scale)
        return carry

    lax.fori_loop(SPATIAL // 32, EXT // 32, normalize_at, 0)
    for gather in key_value:
        gather.spread()

    @pl.when(place["y"] == 3)
    def _():
        halo_copy.start()

    for gather in key_value:
        gather.rise()
        gather.hand(0)

    for number in range(4):
        for gather in key_value:
            gather.rows[number].relay()
    for gather in query_part:
        gather.spread()
    for gather in out_part:
        gather.spread(False)
    for gather in key_value:
        gather.hand(1)
        gather.hand(2)
    for gather in key_value:
        gather.close()
        gather.hand(3)
    for gather in query_part:
        gather.rise()
        gather.hand(0)
    wires.receive(halo_slot, halo, (vid, before))
    lax.fori_loop(0, SPATIAL // 32, normalize_at, 0)
    project(normed, 0, EXT, key_w, core, key_partial, None)
    project(normed, 0, EXT, value_w, core, value_partial, None)
    for gather in key_value:
        gather.take()
    for gather in query_part:
        gather.relay()
        gather.hand(1)
        gather.hand(2)
    project(normed, 0, EXT, key_w, 1 - core, key_partial, key)
    project(normed, 0, EXT, value_w, 1 - core, value_partial, value)

    limit = frames_valid[vid]
    first_frame = tm * FRAMES_DEV
    valid = [
        (first_frame + f - 1 < limit) & (first_frame + f - 1 >= 0) for f in range(FRAMES_DEV + 1)
    ]
    memories = []
    for source, taps, spread, ref in (
        (key, key_taps, spread_key, memory_key),
        (value, value_taps, spread_value, memory_value),
    ):
        pool(source, taps, valid, spread, ref, place)
        region = memory_view(ref, place, 0, WIDTH)
        slot = wires.slot()
        mine, other = (
            [
                Memory(wires, ref, place, core, order, number * HALF, own_plane)
                for number, order in enumerate(MEMORY_ORDERS)
            ]
            for own_plane in (True, False)
        )
        wires.send(slot, region, region, across)
        for part in mine:
            part.first.open()
        memories.append((ref, slot, mine, other))
        if ref is memory_key:
            for gather in query_part:
                gather.close()
                gather.hand(3)
    for gather in out_part:
        gather.rise(False)
        gather.last()
        gather.hand(0)

    (key_ref, key_slot, key_mine, key_other), (value_ref, value_slot, value_mine, value_other) = memories
    far_place = moved(place, "z", 2)
    for part in key_mine:
        part.first.close()
        part.second.open()
    wires.receive(key_slot, memory_view(key_ref, far_place, 0, WIDTH), across)
    for part in key_other:
        part.first.open()
    for part in value_mine:
        part.first.close()
    wires.receive(value_slot, memory_view(value_ref, far_place, 0, WIDTH), across)
    for part in value_other:
        part.first.open()
    for part in key_other:
        part.first.close()
        part.second.open()
    for part in value_mine:
        part.second.open()
    for part in key_mine:
        part.second.relay()
    for gather in query_part:
        gather.take()
    project(normed, SPATIAL, ROWS, query_w, core, key_partial, None)
    for part in value_other:
        part.first.close()
        part.second.open()
    for part in key_other:
        part.second.relay()
    project(normed, SPATIAL, ROWS, query_w, 1 - core, key_partial, query)
    for part in value_mine:
        part.second.relay()
    for gather in out_part:
        gather.relay()
        gather.hand(1)
        gather.hand(2)
    for part in key_mine + key_other:
        part.second.close()

    query_frame = lax.broadcasted_iota(jnp.int32, (ROWS, ROWS), 0) // SPATIAL
    key_frame = lax.broadcasted_iota(jnp.int32, (ROWS, ROWS), 1) // SPATIAL
    near = (key_frame <= query_frame) & (first_frame + key_frame < limit)
    near_bias = jnp.where(near, 0.0, NEG)
    index = lax.broadcasted_iota(jnp.int32, (1, N_TM * MEM_DEV), 1)
    far = (2 * (index // (SPATIAL // 4)) < limit) & (index // MEM_DEV <= tm)
    far_bias = jnp.where(far, 0.0, NEG)

    def weigh(h, carry):
        lanes = pl.ds(pl.multiple_of(h * HD, HD), HD)
        queries = query[:, lanes]
        far_keys = memory_key[:, :, :, :, lanes].reshape(N_TM * MEM_DEV, HD)
        near_scores = scores_of(queries, key[SPATIAL:, lanes]) * SCALE + near_bias
        far_scores = scores_of(queries, far_keys) * SCALE + far_bias
        top = jnp.maximum(
            jnp.max(near_scores, axis=-1, keepdims=True),
            jnp.max(far_scores, axis=-1, keepdims=True),
        )
        total = jnp.zeros((ROWS, 1), jnp.float32)
        for first, scores in ((0, near_scores), (ROWS, far_scores)):
            exps = jnp.exp2(scores - top)
            total = total + jnp.sum(exps, axis=-1, keepdims=True)
            shares[h, :, first : first + scores.shape[1]] = exps.astype(jnp.bfloat16)
        totals[h] = jnp.broadcast_to(total, (ROWS, HD))
        return carry

    lax.fori_loop(0, HEADS // 2, weigh, 0, unroll=4)
    for part in value_other:
        part.second.relay()
    lax.fori_loop(HEADS // 2, HEADS, weigh, 0, unroll=4)

    for gather in out_part:
        gather.close()
        gather.hand(3)
    for gather in out_part:
        gather.take()

    def out_tile(j, carry):
        columns = pl.ds(pl.multiple_of(j * 256, 256), 256)
        out_rows[:, columns] = (
            out_w[:, :, :, :, :, :, columns]
            .astype(jnp.float32)
            .reshape(WIDTH, 256)
            .astype(jnp.bfloat16)
        )
        return carry

    lax.fori_loop(0, D // 256, out_tile, 0, unroll=4)

    for part in value_mine + value_other:
        part.second.close()

    def mix(h, carry):
        lanes = pl.ds(pl.multiple_of(h * HD, HD), HD)
        near_values = value[SPATIAL:, lanes]
        far_values = memory_value[:, :, :, :, lanes].reshape(N_TM * MEM_DEV, HD)
        mixed = jnp.dot(shares[h, :, :ROWS], near_values, preferred_element_type=jnp.float32)
        mixed = mixed + jnp.dot(
            shares[h, :, ROWS:], far_values, preferred_element_type=jnp.float32
        )
        heads[:, lanes] = (mixed / totals[h]).astype(jnp.bfloat16)
        return carry

    lax.fori_loop(0, HEADS, mix, 0, unroll=8)
    row_frame = first_frame + lax.broadcasted_iota(jnp.int32, (ROWS, 1), 0) // SPATIAL

    def result_tile(j, carry):
        columns = pl.ds(pl.multiple_of(j * 512, 512), 512)
        result = jnp.dot(heads[...], out_rows[:, columns], preferred_element_type=jnp.float32)
        out[:, columns] = jnp.where(row_frame < limit, result, 0.0).astype(jnp.bfloat16)
        return carry

    lax.fori_loop(0, D // 512, result_tile, 0, unroll=4)
    wires.drain()


N_SLOTS = len(PIECES) * 26 + 1 + 2 * (1 + 4 * 7)


def on_device(
    video,
    norm_gain,
    query_weight,
    key_weight,
    value_weight,
    key_kernel,
    value_kernel,
    out_weight,
    frames_valid,
):
    bf16 = jnp.bfloat16
    gathered = (2, 2, 4, 2, 4)
    vmem = pl.BlockSpec(memory_space=pltpu.VMEM)
    hbm = pl.BlockSpec(memory_space=pl.ANY)
    result = pl.pallas_call(
        body,
        out_shape=jax.ShapeDtypeStruct((ROWS, D), bf16),
        in_specs=[
            hbm,
            vmem,
            hbm,
            hbm,
            hbm,
            vmem,
            vmem,
            hbm,
            pl.BlockSpec(memory_space=pltpu.SMEM),
        ],
        out_specs=vmem,
        scratch_shapes=[
            pltpu.VMEM((EXT, D), bf16),
            pltpu.VMEM((EXT, D), bf16),
            pltpu.VMEM((*gathered, 16, WIDTH), bf16),
            pltpu.VMEM((*gathered, 16, WIDTH), bf16),
            pltpu.VMEM((*gathered, 16, WIDTH), bf16),
            pltpu.VMEM((*gathered, 8, D), bf16),
            pltpu.VMEM((WIDTH, D), bf16),
            pltpu.VMEM((EXT, WIDTH), jnp.float32),
            pltpu.VMEM((EXT, WIDTH), jnp.float32),
            pltpu.VMEM((ROWS, WIDTH), bf16),
            pltpu.VMEM((EXT, WIDTH), bf16),
            pltpu.VMEM((EXT, WIDTH), bf16),
            pltpu.VMEM((4, 2, 4, MEM_DEV, WIDTH), bf16),
            pltpu.VMEM((4, 2, 4, MEM_DEV, WIDTH), bf16),
            pltpu.VMEM((HEADS, 2 * MEM_DEV, HD), jnp.float32),
            pltpu.VMEM((HEADS, 2 * MEM_DEV, HD), jnp.float32),
            pltpu.VMEM((HEADS, ROWS, KEYS), bf16),
            pltpu.VMEM((HEADS, ROWS, HD), jnp.float32),
            pltpu.VMEM((ROWS, WIDTH), bf16),
            pltpu.SemaphoreType.DMA((5,)),
            pltpu.SemaphoreType.DMA((N_SLOTS,)),
            pltpu.SemaphoreType.DMA((N_SLOTS,)),
        ],
        compiler_params=pltpu.CompilerParams(
            collective_id=0, has_side_effects=True, vmem_limit_bytes=60 * 1024 * 1024
        ),
        name="memory_attention",
    )(
        video[0],
        norm_gain,
        query_weight,
        key_weight,
        value_weight,
        key_kernel,
        value_kernel,
        out_weight,
        frames_valid,
    )
    return result[None]


def solution(mesh):
    in_specs = (
        P("vid", "tm", None),
        P(),
        P(("vid", "tm"), None),
        P(("vid", "tm"), None),
        P(("vid", "tm"), None),
        P(),
        P(),
        P(("vid", "tm"), None),
        P(),
    )
    out_specs = P("vid", "tm", None)
    return jax.shard_map(
        on_device, mesh=mesh, in_specs=in_specs, out_specs=out_specs, check_vma=False
    )
```
